256 devices in a mesh: ctx: 64 (over z, y, core), pipe: 4 (over x).
Axes of the slice: x: 4, y: 4, z: 8, core: 2. Of those that a mesh axis runs over, the one named last changes fastest.
Arguments:
- queries: bfloat16 [4, 32768, 2048], P('pipe', 'ctx'), may hold values from -400 to 400
- keys: bfloat16 [4, 32768, 2048], P('pipe', 'ctx'), may hold values from -12 to 12
- values: bfloat16 [4, 32768, 2048], P('pipe', 'ctx'), may hold values from -15 to 15
- picks: int32 [4, 64, 16, 2], P('pipe'), may hold values from -1 to 62, as said below
Outputs:
- passed: bfloat16 [4, 32768, 2048], P('pipe', 'ctx')
The draws below stay inside these ranges and needn't reach their ends.
Inputs may be any that keep to these rules, and one draw needn't show every extreme that they name: Each entry is -1 (no block) or a block earlier than its query block; a head's 2 entries differ unless -1; within one section and query block no block is named more than 1 times over all heads and picks, and this bound is reached; query block 0 names nothing and every later query block names its preceding block at least once.
All inputs are finite; a program needn't handle non-finite values.
Results may differ from the reference program's by a relative error of at most 0.0048.
Values may be sent and summed in bfloat16 or wider, within the bound.
A program may use at most 128 MiB of HBM per device.

```python
import jax
import jax.numpy as jnp
from jax import lax

HEADS = 16
HD = 128
D = 2048
BLOCK = 512
PICKS = 2
NB = 64
TOKENS = 32768
CAP = 1
N_PIPE = 4


def shared_draw(key):
    base_key = jax.random.fold_in(key, 1013)
    key_first, key_second = jax.random.split(base_key, 2)
    full_shape = (N_PIPE, TOKENS, D)
    key_part = jax.random.truncated_normal(key_first, -4.0, 4.0, full_shape, jnp.float32)
    query_part = 2.0 * jax.random.truncated_normal(key_second, -4.0, 4.0, full_shape, jnp.float32)
    return (query_part, key_part)


def draw_queries(key, part):
    return shared_draw(key)[0].astype(jnp.bfloat16)


def draw_keys(key, part):
    return shared_draw(key)[1].astype(jnp.bfloat16)


def pick_block(layer_key, block_index):
    block_key = jax.random.fold_in(layer_key, block_index)
    key_order, key_heads = jax.random.split(block_key)
    owner_ids = lax.iota(jnp.int32, NB)
    noise = jax.random.randint(key_order, (NB,), 0, 1 << 20) * NB + owner_ids
    noise = jnp.where(owner_ids == block_index - 1, -1, noise)
    noise = jnp.where(owner_ids < block_index, noise, 1 << 30)
    ranked = jnp.argsort(noise).astype(jnp.int32)
    pick_ids = lax.iota(jnp.int32, HEADS * PICKS)
    is_live = (pick_ids < block_index * CAP) & ((block_index >= 2) | (pick_ids % PICKS == 0))
    chosen = ranked[pick_ids % jnp.maximum(block_index, 1)]
    chosen = jnp.where(is_live, chosen, -1).reshape(HEADS, PICKS)
    shuffle = jax.random.permutation(key_heads, HEADS)
    return chosen[shuffle]


def draw_picks(key, part):
    base_key = jax.random.fold_in(key, 2027)

    def one_layer(layer_index):
        layer_key = jax.random.fold_in(base_key, layer_index)
        return jax.vmap(lambda block_index: pick_block(layer_key, block_index))(lax.iota(jnp.int32, NB))
    return jax.vmap(one_layer)(lax.iota(jnp.int32, N_PIPE))


def block_scale(rng, shape, cuts, least, largest):
    def one(dim, parts):
        steps = jax.random.uniform(jax.random.fold_in(jax.random.fold_in(rng, 6), dim), (parts,), jnp.float32, least / len(cuts), largest / len(cuts))
        return jnp.repeat(jnp.exp(steps), shape[dim] // parts).reshape((-1,) + (1,) * (len(shape) - dim - 1))

    loudness = one(*cuts[0])
    for cut in cuts[1:]:
        loudness = loudness * one(*cut)
    return loudness


def scatter_about(stream_key, extent, scale, reach, cuts=(), kind=jnp.bfloat16):
    values = scale * jax.random.normal(stream_key, extent, jnp.float32)
    if cuts:
        values = values * block_scale(stream_key, extent, cuts, -0.22, 0.18)
    return jnp.clip(values, -reach, reach).astype(kind)


def setup_inputs(seed: int = 0) -> dict:
    key_list = jax.random.split(jax.random.key(seed), 5)
    return {
        "queries": draw_queries(jax.random.fold_in(key_list[4], 71), 0),
        "keys": draw_keys(jax.random.fold_in(key_list[4], 71), 0),
        "values": scatter_about(key_list[2], (N_PIPE, TOKENS, D), 3.0, 15.0, ((0, 4), (1, 64))),
        "picks": draw_picks(jax.random.fold_in(key_list[4], 71), 0),
    }


def attend_block(query_rows, key_blocks, value_blocks, chosen, block_index):
    score_scale = HD ** -0.5
    head_index = jnp.arange(HEADS, dtype=jnp.int32)[:, None]
    safe_blocks = jnp.maximum(chosen, 0)
    remote_keys = key_blocks[safe_blocks, :, head_index, :]
    remote_values = value_blocks[safe_blocks, :, head_index, :]
    own_keys = key_blocks[block_index].transpose(1, 0, 2)
    own_values = value_blocks[block_index].transpose(1, 0, 2)
    all_keys = jnp.concatenate([own_keys, remote_keys.reshape(HEADS, PICKS * BLOCK, HD)], axis=1).astype(jnp.float32)
    all_values = jnp.concatenate([own_values, remote_values.reshape(HEADS, PICKS * BLOCK, HD)], axis=1).astype(jnp.float32)
    query_heads = query_rows.reshape(BLOCK, HEADS, HD).transpose(1, 0, 2).astype(jnp.float32)
    scores = jnp.einsum("hqd,hkd->hqk", query_heads, all_keys, precision=lax.Precision.HIGHEST) * score_scale
    positions = jnp.arange(BLOCK, dtype=jnp.int32)
    causal = positions[:, None] >= positions[None, :]
    remote_mask = jnp.repeat(chosen >= 0, BLOCK, axis=1)
    allowed = jnp.concatenate([jnp.broadcast_to(causal[None], (HEADS, BLOCK, BLOCK)), jnp.broadcast_to(remote_mask[:, None, :], (HEADS, BLOCK, PICKS * BLOCK))], axis=2)
    scores = jnp.where(allowed, scores, -jnp.inf)
    row_top = jnp.max(scores, axis=2, keepdims=True)
    weights = jnp.exp(scores - row_top)
    prob_rows = (weights / jnp.sum(weights, axis=2, keepdims=True)).astype(jnp.bfloat16)
    prob_rows = lax.optimization_barrier(prob_rows).astype(jnp.float32)
    mixed_rows = jnp.einsum("hqk,hkd->hqd", prob_rows, all_values, precision=lax.Precision.HIGHEST)
    return mixed_rows.astype(jnp.bfloat16).transpose(1, 0, 2).reshape(BLOCK, HEADS * HD)


def reference(queries, keys, values, picks):
    sections = []
    for layer_index in range(N_PIPE):
        key_blocks = keys[layer_index].reshape(NB, BLOCK, HEADS, HD)
        value_blocks = values[layer_index].reshape(NB, BLOCK, HEADS, HD)
        query_blocks = queries[layer_index].reshape(NB, BLOCK, HEADS * HD)

        def one_block(block_items, key_blocks=key_blocks, value_blocks=value_blocks):
            query_rows, chosen, block_index = block_items
            return attend_block(query_rows, key_blocks, value_blocks, chosen, block_index)

        attended = lax.map(one_block, (query_blocks, picks[layer_index], jnp.arange(NB, dtype=jnp.int32)))
        sections.append(attended.reshape(TOKENS, HEADS * HD))
    stacked = jnp.stack(sections)
    return jnp.roll(stacked, 1, axis=0)
```

```python
import functools

import jax
import jax.numpy as jnp
from jax import lax
from jax.experimental import pallas as pl
from jax.experimental.pallas import tpu as pltpu
from jax.sharding import PartitionSpec as P

HEADS = 16
HD = 128
PICKS = 2
MESH = pl.DeviceIdType.MESH


def passed_along(value, axis, steps):
    count = lax.axis_size(axis)
    pairs = [(source, (source + steps) % count) for source in range(count)]
    return lax.ppermute(value, axis, pairs)


def pack_kernel(asked_ref, k_ref, v_ref, out_ref):
    out_ref[0, 0] = k_ref[...]
    out_ref[0, 1] = v_ref[...]


def pack_requested(asked, keys, values):
    count = asked.shape[0]
    rows = keys.shape[0]
    grid_spec = pltpu.PrefetchScalarGridSpec(
        num_scalar_prefetch=1,
        grid=(count,),
        in_specs=[
            pl.BlockSpec((rows, HD), lambda q, asked_ref: (0, asked_ref[q])),
            pl.BlockSpec((rows, HD), lambda q, asked_ref: (0, asked_ref[q])),
        ],
        out_specs=pl.BlockSpec((1, 2, rows, HD), lambda q, asked_ref: (q, 0, 0, 0)),
    )
    return pl.pallas_call(
        pack_kernel,
        grid_spec=grid_spec,
        out_shape=jax.ShapeDtypeStruct((count, 2, rows, HD), keys.dtype),
    )(asked, keys, values)


def exchange_kernel(count, send_ref, recv_ref, send_sems, recv_sems):
    me = lax.axis_index("ctx")
    barrier = pltpu.get_barrier_semaphore()

    def greet(step, carry):
        peer = lax.rem(me + step, count)
        pl.semaphore_signal(barrier, 1, device_id={"ctx": peer}, device_id_type=MESH)
        return carry

    lax.fori_loop(1, count, greet, 0)
    pl.semaphore_wait(barrier, count - 1)

    def copy_between(source, target, slot):
        return pltpu.make_async_remote_copy(
            src_ref=send_ref.at[slot],
            dst_ref=recv_ref.at[source],
            send_sem=send_sems.at[slot],
            recv_sem=recv_sems.at[source],
            device_id={"ctx": target},
            device_id_type=MESH,
        )

    def start(step, carry):
        target = me + step

        @pl.when(target < count)
        def _():
            copy_between(me, target, target).start()

        return carry

    lax.fori_loop(1, count, start, 0)

    def finish(peer, carry):
        @pl.when(peer > me)
        def _():
            copy_between(me, peer, peer).wait_send()

        @pl.when(peer < me)
        def _():
            copy_between(peer, peer, peer).wait_recv()

        return carry

    lax.fori_loop(0, count, finish, 0)


def exchange(send):
    count = send.shape[0]
    return pl.pallas_call(
        functools.partial(exchange_kernel, count),
        out_shape=jax.ShapeDtypeStruct(send.shape, send.dtype),
        in_specs=[pl.BlockSpec(memory_space=pl.ANY)],
        out_specs=pl.BlockSpec(memory_space=pl.ANY),
        scratch_shapes=[
            pltpu.SemaphoreType.DMA((count,)),
            pltpu.SemaphoreType.DMA((count,)),
        ],
        compiler_params=pltpu.CompilerParams(collective_id=0, has_side_effects=True),
    )(send)


def attend_kernel(slot_ref, live_ref, q_ref, k_ref, v_ref, first_ref, second_ref, o_ref):
    head = pl.program_id(0)
    rows = q_ref.shape[0]
    score_scale = HD ** (-0.5)
    dims = (((1,), (1,)), ((), ()))
    query = q_ref[...]

    def scores_against(key_rows):
        raw = lax.dot_general(query, key_rows, dims, preferred_element_type=jnp.float32)
        return raw * score_scale

    row_index = lax.broadcasted_iota(jnp.int32, (rows, rows), 0)
    col_index = lax.broadcasted_iota(jnp.int32, (rows, rows), 1)
    own = jnp.where(row_index >= col_index, scores_against(k_ref[...]), -jnp.inf)
    live_first = live_ref[PICKS * head] > 0
    live_second = live_ref[PICKS * head + 1] > 0
    first = jnp.where(live_first, scores_against(first_ref[0, 0]), -jnp.inf)
    second = jnp.where(live_second, scores_against(second_ref[0, 0]), -jnp.inf)
    row_top = jnp.maximum(
        jnp.maximum(jnp.max(own, axis=1), jnp.max(first, axis=1)), jnp.max(second, axis=1)
    )[:, None]
    own = jnp.exp(own - row_top)
    first = jnp.exp(first - row_top)
    second = jnp.exp(second - row_top)
    row_total = (
        jnp.sum(own, axis=1) + jnp.sum(first, axis=1) + jnp.sum(second, axis=1)
    )[:, None]
    first_values = jnp.where(live_first, first_ref[0, 1], jnp.zeros_like(first_ref[0, 1]))
    second_values = jnp.where(live_second, second_ref[0, 1], jnp.zeros_like(second_ref[0, 1]))
    mixed = jnp.dot((own / row_total).astype(jnp.bfloat16), v_ref[...],
                    preferred_element_type=jnp.float32)
    mixed += jnp.dot((first / row_total).astype(jnp.bfloat16), first_values,
                     preferred_element_type=jnp.float32)
    mixed += jnp.dot((second / row_total).astype(jnp.bfloat16), second_values,
                     preferred_element_type=jnp.float32)
    o_ref[...] = mixed.astype(o_ref.dtype)


def attend(slots, live, queries, keys, values, received):
    rows = queries.shape[0]
    head_block = pl.BlockSpec((rows, HD), lambda h, slot_ref, live_ref: (0, h))
    grid_spec = pltpu.PrefetchScalarGridSpec(
        num_scalar_prefetch=2,
        grid=(HEADS,),
        in_specs=[
            head_block,
            head_block,
            head_block,
            pl.BlockSpec(
                (1, 2, rows, HD), lambda h, slot_ref, live_ref: (slot_ref[PICKS * h], 0, 0, 0)
            ),
            pl.BlockSpec(
                (1, 2, rows, HD),
                lambda h, slot_ref, live_ref: (slot_ref[PICKS * h + 1], 0, 0, 0),
            ),
        ],
        out_specs=head_block,
    )
    return pl.pallas_call(
        attend_kernel,
        grid_spec=grid_spec,
        out_shape=jax.ShapeDtypeStruct(queries.shape, queries.dtype),
    )(slots, live, queries, keys, values, received, received)


def per_device(queries, keys, values, picks):
    rank_here = lax.axis_index("ctx")
    every_pick = picks[0]
    head_ids = lax.broadcasted_iota(jnp.int32, every_pick.shape, 1)
    asked = jnp.sum(jnp.where(every_pick == rank_here, head_ids, 0), axis=(1, 2))
    send = pack_requested(asked.astype(jnp.int32), keys[0], values[0])
    received = exchange(send)
    chosen = lax.dynamic_index_in_dim(every_pick, rank_here, 0, keepdims=False).reshape(-1)
    live = (chosen >= 0).astype(jnp.int32)
    slots = jnp.maximum(chosen, 0).astype(jnp.int32)
    merged = attend(slots, live, queries[0], keys[0], values[0], received)
    merged = passed_along(merged[None], "pipe", 1)
    return merged


def solution(mesh):
    placed = (
        P("pipe", "ctx", None),
        P("pipe", "ctx", None),
        P("pipe", "ctx", None),
        P("pipe", None, None, None),
    )
    return jax.shard_map(
        per_device, mesh=mesh, in_specs=placed, out_specs=P("pipe", "ctx", None), check_vma=False
    )
```

```python
import functools

import jax
import jax.numpy as jnp
from jax import lax
from jax.experimental import pallas as pl
from jax.experimental.pallas import tpu as pltpu
from jax.sharding import PartitionSpec as P

HEADS = 16
HD = 128
PICKS = 2
MESH = pl.DeviceIdType.MESH


def passed_along(value, axis, steps):
    count = lax.axis_size(axis)
    pairs = [(source, (source + steps) % count) for source in range(count)]
    return lax.ppermute(value, axis, pairs)


def pack_kernel(group, asked_ref, k_ref, v_ref, out_ref):
    base = pl.program_id(0) * group
    for i in range(group):
        column = pl.multiple_of(asked_ref[base + i] * HD, HD)
        out_ref[i, 0] = k_ref[:, pl.ds(column, HD)]
        out_ref[i, 1] = v_ref[:, pl.ds(column, HD)]


def pack_requested(asked, keys, values):
    count = asked.shape[0]
    rows, width = keys.shape
    group = 8
    whole = pl.BlockSpec((rows, width), lambda g, asked_ref: (0, 0))
    grid_spec = pltpu.PrefetchScalarGridSpec(
        num_scalar_prefetch=1,
        grid=(count // group,),
        in_specs=[whole, whole],
        out_specs=pl.BlockSpec((group, 2, rows, HD), lambda g, asked_ref: (g, 0, 0, 0)),
    )
    return pl.pallas_call(
        functools.partial(pack_kernel, group),
        grid_spec=grid_spec,
        out_shape=jax.ShapeDtypeStruct((count, 2, rows, HD), keys.dtype),
    )(asked, keys, values)


def exchange_kernel(count, send_ref, recv_ref, send_sems, recv_sems):
    me = lax.axis_index("ctx")
    barrier = pltpu.get_barrier_semaphore()

    def greet(step, carry):
        peer = lax.rem(me + step, count)
        pl.semaphore_signal(barrier, 1, device_id={"ctx": peer}, device_id_type=MESH)
        return carry

    lax.fori_loop(1, count, greet, 0)
    pl.semaphore_wait(barrier, count - 1)

    def copy_between(source, target, slot):
        return pltpu.make_async_remote_copy(
            src_ref=send_ref.at[slot],
            dst_ref=recv_ref.at[source],
            send_sem=send_sems.at[slot],
            recv_sem=recv_sems.at[source],
            device_id={"ctx": target},
            device_id_type=MESH,
        )

    def start(step, carry):
        target = me + step

        @pl.when(target < count)
        def _():
            copy_between(me, target, target).start()

        return carry

    lax.fori_loop(1, count, start, 0)

    def finish(peer, carry):
        @pl.when(peer > me)
        def _():
            copy_between(me, peer, peer).wait_send()

        @pl.when(peer < me)
        def _():
            copy_between(peer, peer, peer).wait_recv()

        return carry

    lax.fori_loop(0, count, finish, 0)


def exchange(send):
    count = send.shape[0]
    return pl.pallas_call(
        functools.partial(exchange_kernel, count),
        out_shape=jax.ShapeDtypeStruct(send.shape, send.dtype),
        in_specs=[pl.BlockSpec(memory_space=pl.ANY)],
        out_specs=pl.BlockSpec(memory_space=pl.ANY),
        scratch_shapes=[
            pltpu.SemaphoreType.DMA((count,)),
            pltpu.SemaphoreType.DMA((count,)),
        ],
        compiler_params=pltpu.CompilerParams(collective_id=0, has_side_effects=True),
    )(send)


def attend_kernel(slot_ref, live_ref, q_ref, k_ref, v_ref, first_ref, second_ref, o_ref):
    head = pl.program_id(0)
    rows = q_ref.shape[0]
    score_scale = HD ** (-0.5)
    dims = (((1,), (1,)), ((), ()))
    query = q_ref[...]

    def scores_against(key_rows):
        raw = lax.dot_general(query, key_rows, dims, preferred_element_type=jnp.float32)
        return raw * score_scale

    row_index = lax.broadcasted_iota(jnp.int32, (rows, rows), 0)
    col_index = lax.broadcasted_iota(jnp.int32, (rows, rows), 1)
    own = jnp.where(row_index >= col_index, scores_against(k_ref[...]), -jnp.inf)
    live_first = live_ref[PICKS * head] > 0
    live_second = live_ref[PICKS * head + 1] > 0
    first = jnp.where(live_first, scores_against(first_ref[0, 0]), -jnp.inf)
    second = jnp.where(live_second, scores_against(second_ref[0, 0]), -jnp.inf)
    row_top = jnp.maximum(
        jnp.maximum(jnp.max(own, axis=1), jnp.max(first, axis=1)), jnp.max(second, axis=1)
    )[:, None]
    own = jnp.exp(own - row_top)
    first = jnp.exp(first - row_top)
    second = jnp.exp(second - row_top)
    row_scale = 1.0 / (
        jnp.sum(own, axis=1) + jnp.sum(first, axis=1) + jnp.sum(second, axis=1)
    )[:, None]
    first_values = jnp.where(live_first, first_ref[0, 1], jnp.zeros_like(first_ref[0, 1]))
    second_values = jnp.where(live_second, second_ref[0, 1], jnp.zeros_like(second_ref[0, 1]))
    mixed = jnp.dot((own * row_scale).astype(jnp.bfloat16), v_ref[...],
                    preferred_element_type=jnp.float32)
    mixed += jnp.dot((first * row_scale).astype(jnp.bfloat16), first_values,
                     preferred_element_type=jnp.float32)
    mixed += jnp.dot((second * row_scale).astype(jnp.bfloat16), second_values,
                     preferred_element_type=jnp.float32)
    o_ref[...] = mixed.astype(o_ref.dtype)


def attend(slots, live, queries, keys, values, received):
    rows = queries.shape[0]
    head_block = pl.BlockSpec((rows, HD), lambda h, slot_ref, live_ref: (0, h))
    grid_spec = pltpu.PrefetchScalarGridSpec(
        num_scalar_prefetch=2,
        grid=(HEADS,),
        in_specs=[
            head_block,
            head_block,
            head_block,
            pl.BlockSpec(
                (1, 2, rows, HD), lambda h, slot_ref, live_ref: (slot_ref[PICKS * h], 0, 0, 0)
            ),
            pl.BlockSpec(
                (1, 2, rows, HD),
                lambda h, slot_ref, live_ref: (slot_ref[PICKS * h + 1], 0, 0, 0),
            ),
        ],
        out_specs=head_block,
    )
    return pl.pallas_call(
        attend_kernel,
        grid_spec=grid_spec,
        out_shape=jax.ShapeDtypeStruct(queries.shape, queries.dtype),
    )(slots, live, queries, keys, values, received, received)


def per_device(queries, keys, values, picks):
    rank_here = lax.axis_index("ctx")
    every_pick = picks[0]
    head_ids = lax.broadcasted_iota(jnp.int32, every_pick.shape, 1)
    asked = jnp.sum(jnp.where(every_pick == rank_here, head_ids, 0), axis=(1, 2))
    send = pack_requested(asked.astype(jnp.int32), keys[0], values[0])
    received = lax.all_to_all(send, "ctx", split_axis=0, concat_axis=0, tiled=True)
    chosen = lax.dynamic_index_in_dim(every_pick, rank_here, 0, keepdims=False).reshape(-1)
    live = (chosen >= 0).astype(jnp.int32)
    slots = jnp.maximum(chosen, 0).astype(jnp.int32)
    merged = attend(slots, live, queries[0], keys[0], values[0], received)
    merged = passed_along(merged[None], "pipe", 1)
    return merged


def solution(mesh):
    placed = (
        P("pipe", "ctx", None),
        P("pipe", "ctx", None),
        P("pipe", "ctx", None),
        P("pipe", None, None, None),
    )
    return jax.shard_map(
        per_device, mesh=mesh, in_specs=placed, out_specs=P("pipe", "ctx", None), check_vma=False
    )
```

```python
import functools

import jax
import jax.numpy as jnp
from jax import lax
from jax.experimental import pallas as pl
from jax.experimental.pallas import tpu as pltpu
from jax.sharding import PartitionSpec as P

HEADS = 16
HD = 128
PICKS = 2
MESH = pl.DeviceIdType.MESH


def passed_along(value, axis, steps):
    count = lax.axis_size(axis)
    pairs = [(source, (source + steps) % count) for source in range(count)]
    return lax.ppermute(value, axis, pairs)


def pack_kernel(group, count_in, wanted_ref, *refs):
    sources, out_ref = refs[:count_in], refs[count_in]
    base = pl.program_id(0) * group
    for i in range(group):
        column = pl.multiple_of(wanted_ref[base + i] * HD, HD)
        for j, source in enumerate(sources):
            out_ref[i, j] = source[:, pl.ds(column, HD)]


def pack_heads(wanted, *sources):
    count = wanted.shape[0]
    rows, width = sources[0].shape
    group = 8
    whole = pl.BlockSpec((rows, width), lambda g, wanted_ref: (0, 0))
    grid_spec = pltpu.PrefetchScalarGridSpec(
        num_scalar_prefetch=1,
        grid=(count // group,),
        in_specs=[whole] * len(sources),
        out_specs=pl.BlockSpec(
            (group, len(sources), rows, HD), lambda g, wanted_ref: (g, 0, 0, 0)
        ),
    )
    return pl.pallas_call(
        functools.partial(pack_kernel, group, len(sources)),
        grid_spec=grid_spec,
        out_shape=jax.ShapeDtypeStruct((count, len(sources), rows, HD), sources[0].dtype),
    )(wanted, *sources)


def partial_kernel(count, query_out_ref, kv_ref, part_ref, stat_ref, query_in, part_out,
                   stat_out, query_sems, part_sems, stat_sems):
    me = lax.axis_index("ctx")
    rows = part_ref.shape[1]
    score_scale = HD ** (-0.5)
    dims = (((1,), (1,)), ((), ()))
    barrier = pltpu.get_barrier_semaphore()

    def greet(step, carry):
        peer = lax.rem(me + step, count)
        pl.semaphore_signal(barrier, 1, device_id={"ctx": peer}, device_id_type=MESH)
        return carry

    lax.fori_loop(1, count, greet, 0)
    pl.semaphore_wait(barrier, count - 1)

    def query_copy(source, target):
        return pltpu.make_async_remote_copy(
            src_ref=query_out_ref.at[target, 0],
            dst_ref=query_in.at[source],
            send_sem=query_sems.at[0, target],
            recv_sem=query_sems.at[1, source],
            device_id={"ctx": target},
            device_id_type=MESH,
        )

    def part_copy(source, target):
        return pltpu.make_async_remote_copy(
            src_ref=part_out.at[target],
            dst_ref=part_ref.at[source],
            send_sem=part_sems.at[0, target],
            recv_sem=part_sems.at[1, source],
            device_id={"ctx": target},
            device_id_type=MESH,
        )

    def stat_copy(source, target):
        return pltpu.make_async_remote_copy(
            src_ref=stat_out.at[target],
            dst_ref=stat_ref.at[source],
            send_sem=stat_sems.at[0, target],
            recv_sem=stat_sems.at[1, source],
            device_id={"ctx": target},
            device_id_type=MESH,
        )

    def ask(step, carry):
        owner = me - step

        @pl.when(owner >= 0)
        def _():
            query_copy(me, owner).start()

        return carry

    lax.fori_loop(1, count, ask, 0)

    def serve(step, carry):
        asker = me + step

        @pl.when(asker < count)
        def _():
            query_copy(asker, me).wait_recv()
            scores = lax.dot_general(
                query_in[asker], kv_ref[asker, 0], dims, preferred_element_type=jnp.float32
            ) * score_scale
            row_top = jnp.max(scores, axis=1, keepdims=True)
            weights = jnp.exp(scores - row_top)
            row_total = jnp.sum(weights, axis=1, keepdims=True)
            mixed = jnp.dot(weights.astype(jnp.bfloat16), kv_ref[asker, 1],
                            preferred_element_type=jnp.float32)
            part_out[asker] = mixed.astype(part_out.dtype)
            stats = jnp.concatenate(
                [row_top, row_total, jnp.zeros((rows, 6), jnp.float32)], axis=1
            )
            stat_out[asker] = stats.T
            part_copy(me, asker).start()
            stat_copy(me, asker).start()

        return carry

    lax.fori_loop(1, count, serve, 0)

    def finish(peer, carry):
        @pl.when(peer < me)
        def _():
            query_copy(me, peer).wait_send()
            part_copy(peer, me).wait_recv()
            stat_copy(peer, me).wait_recv()

        @pl.when(peer > me)
        def _():
            part_copy(me, peer).wait_send()
            stat_copy(me, peer).wait_send()

        return carry

    lax.fori_loop(0, count, finish, 0)


def partials(query_out, kv):
    count, _, rows, _ = kv.shape
    return pl.pallas_call(
        functools.partial(partial_kernel, count),
        out_shape=(
            jax.ShapeDtypeStruct((count, rows, HD), kv.dtype),
            jax.ShapeDtypeStruct((count, 8, rows), jnp.float32),
        ),
        in_specs=[
            pl.BlockSpec(memory_space=pl.ANY),
            pl.BlockSpec(memory_space=pltpu.VMEM),
        ],
        out_specs=(pl.BlockSpec(memory_space=pl.ANY), pl.BlockSpec(memory_space=pl.ANY)),
        scratch_shapes=[
            pltpu.VMEM((count, rows, HD), kv.dtype),
            pltpu.VMEM((count, rows, HD), kv.dtype),
            pltpu.VMEM((count, 8, rows), jnp.float32),
            pltpu.SemaphoreType.DMA((2, count)),
            pltpu.SemaphoreType.DMA((2, count)),
            pltpu.SemaphoreType.DMA((2, count)),
        ],
        compiler_params=pltpu.CompilerParams(
            collective_id=0, has_side_effects=True, vmem_limit_bytes=60 * 1024 * 1024
        ),
    )(query_out, kv)


def attend_kernel(slot_ref, live_ref, q_ref, k_ref, v_ref, first_ref, second_ref,
                  first_stat_ref, second_stat_ref, o_ref):
    head = pl.program_id(0)
    rows = q_ref.shape[0]
    score_scale = HD ** (-0.5)
    dims = (((1,), (1,)), ((), ()))
    raw = lax.dot_general(q_ref[...], k_ref[...], dims, preferred_element_type=jnp.float32)
    row_index = lax.broadcasted_iota(jnp.int32, (rows, rows), 0)
    col_index = lax.broadcasted_iota(jnp.int32, (rows, rows), 1)
    own = jnp.where(row_index >= col_index, raw * score_scale, -jnp.inf)

    def remote(live, part_ref, stat_ref):
        stats = stat_ref[0].T
        top = jnp.where(live, stats[:, 0:1], -jnp.inf)
        total = jnp.where(live, stats[:, 1:2], 0.0)
        part = jnp.where(live, part_ref[0].astype(jnp.float32), 0.0)
        return top, total, part

    first_top, first_total, first_part = remote(live_ref[PICKS * head] > 0, first_ref,
                                                first_stat_ref)
    second_top, second_total, second_part = remote(live_ref[PICKS * head + 1] > 0, second_ref,
                                                   second_stat_ref)
    row_top = jnp.maximum(jnp.maximum(jnp.max(own, axis=1, keepdims=True), first_top),
                          second_top)
    own = jnp.exp(own - row_top)
    first_scale = jnp.exp(first_top - row_top)
    second_scale = jnp.exp(second_top - row_top)
    row_scale = 1.0 / (
        jnp.sum(own, axis=1, keepdims=True) + first_scale * first_total
        + second_scale * second_total
    )
    mixed = jnp.dot((own * row_scale).astype(jnp.bfloat16), v_ref[...],
                    preferred_element_type=jnp.float32)
    mixed += (first_scale * row_scale) * first_part + (second_scale * row_scale) * second_part
    o_ref[...] = mixed.astype(o_ref.dtype)


def attend(slots, live, queries, keys, values, parts, stats):
    rows = queries.shape[0]
    head_block = pl.BlockSpec((rows, HD), lambda h, slot_ref, live_ref: (0, h))

    def picked(j, shape):
        return pl.BlockSpec(
            (1,) + shape, lambda h, slot_ref, live_ref: (slot_ref[PICKS * h + j], 0, 0)
        )

    grid_spec = pltpu.PrefetchScalarGridSpec(
        num_scalar_prefetch=2,
        grid=(HEADS,),
        in_specs=[
            head_block,
            head_block,
            head_block,
            picked(0, (rows, HD)),
            picked(1, (rows, HD)),
            picked(0, (8, rows)),
            picked(1, (8, rows)),
        ],
        out_specs=head_block,
    )
    return pl.pallas_call(
        attend_kernel,
        grid_spec=grid_spec,
        out_shape=jax.ShapeDtypeStruct(queries.shape, queries.dtype),
    )(slots, live, queries, keys, values, parts, parts, stats, stats)


def per_device(queries, keys, values, picks):
    rank_here = lax.axis_index("ctx")
    every_pick = picks[0]
    count = every_pick.shape[0]
    head_ids = lax.broadcasted_iota(jnp.int32, every_pick.shape, 1)
    asked = jnp.sum(jnp.where(every_pick == rank_here, head_ids, 0), axis=(1, 2))
    kv = pack_heads(asked.astype(jnp.int32), keys[0], values[0])
    chosen = lax.dynamic_index_in_dim(every_pick, rank_here, 0, keepdims=False).reshape(-1)
    owners = lax.broadcasted_iota(jnp.int32, (count, HEADS * PICKS), 0)
    wanted = jnp.sum(
        jnp.where(chosen[None, :] == owners, jnp.repeat(lax.iota(jnp.int32, HEADS), PICKS), 0),
        axis=1,
    )
    query_out = pack_heads(wanted.astype(jnp.int32), queries[0])
    parts, stats = partials(query_out, kv)
    live = (chosen >= 0).astype(jnp.int32)
    slots = jnp.maximum(chosen, 0).astype(jnp.int32)
    merged = attend(slots, live, queries[0], keys[0], values[0], parts, stats)
    merged = passed_along(merged[None], "pipe", 1)
    return merged


def solution(mesh):
    placed = (
        P("pipe", "ctx", None),
        P("pipe", "ctx", None),
        P("pipe", "ctx", None),
        P("pipe", None, None, None),
    )
    return jax.shard_map(
        per_device, mesh=mesh, in_specs=placed, out_specs=P("pipe", "ctx", None), check_vma=False
    )
```

```python
import functools

import jax
import jax.numpy as jnp
from jax import lax
from jax.experimental import pallas as pl
from jax.experimental.pallas import tpu as pltpu
from jax.sharding import PartitionSpec as P

HEADS = 16
HD = 128
PICKS = 2
MESH = pl.DeviceIdType.MESH


def passed_along(value, axis, steps):
    count = lax.axis_size(axis)
    pairs = [(source, (source + steps) % count) for source in range(count)]
    return lax.ppermute(value, axis, pairs)


def pack_kernel(group, count_in, wanted_ref, *refs):
    sources, out_ref = refs[:count_in], refs[count_in]
    base = pl.program_id(0) * group
    for i in range(group):
        column = pl.multiple_of(wanted_ref[base + i] * HD, HD)
        for j, source in enumerate(sources):
            out_ref[i, j] = source[:, pl.ds(column, HD)]


def pack_heads(wanted, *sources):
    count = wanted.shape[0]
    rows, width = sources[0].shape
    group = 8
    whole = pl.BlockSpec((rows, width), lambda g, wanted_ref: (0, 0))
    grid_spec = pltpu.PrefetchScalarGridSpec(
        num_scalar_prefetch=1,
        grid=(count // group,),
        in_specs=[whole] * len(sources),
        out_specs=pl.BlockSpec(
            (group, len(sources), rows, HD), lambda g, wanted_ref: (g, 0, 0, 0)
        ),
    )
    return pl.pallas_call(
        functools.partial(pack_kernel, group, len(sources)),
        grid_spec=grid_spec,
        out_shape=jax.ShapeDtypeStruct((count, len(sources), rows, HD), sources[0].dtype),
    )(wanted, *sources)


def partial_kernel(count, query_out_ref, kv_ref, part_ref, stat_ref, query_in, part_out,
                   stat_out, query_sems, part_sems, stat_sems):
    me = lax.axis_index("ctx")
    rows = part_ref.shape[1]
    score_scale = HD ** (-0.5)
    dims = (((1,), (1,)), ((), ()))
    barrier = pltpu.get_barrier_semaphore()

    def greet(step, carry):
        peer = lax.rem(me + step, count)
        pl.semaphore_signal(barrier, 1, device_id={"ctx": peer}, device_id_type=MESH)
        return carry

    lax.fori_loop(1, count, greet, 0)
    pl.semaphore_wait(barrier, count - 1)

    def query_copy(source, target):
        return pltpu.make_async_remote_copy(
            src_ref=query_out_ref.at[target, 0],
            dst_ref=query_in.at[source],
            send_sem=query_sems.at[0, target],
            recv_sem=query_sems.at[1, source],
            device_id={"ctx": target},
            device_id_type=MESH,
        )

    def part_copy(source, target):
        return pltpu.make_async_remote_copy(
            src_ref=part_out.at[target],
            dst_ref=part_ref.at[source],
            send_sem=part_sems.at[0, target],
            recv_sem=part_sems.at[1, source],
            device_id={"ctx": target},
            device_id_type=MESH,
        )

    def stat_copy(source, target):
        return pltpu.make_async_remote_copy(
            src_ref=stat_out.at[target],
            dst_ref=stat_ref.at[source],
            send_sem=stat_sems.at[0, target],
            recv_sem=stat_sems.at[1, source],
            device_id={"ctx": target},
            device_id_type=MESH,
        )

    def ask(owner, carry):
        @pl.when(owner < me)
        def _():
            query_copy(me, owner).start()

        return carry

    lax.fori_loop(0, count, ask, 0)

    def serve(step, carry):
        asker = me + step

        @pl.when(asker < count)
        def _():
            query_copy(asker, me).wait_recv()
            scores = lax.dot_general(
                query_in[asker], kv_ref[asker, 0], dims, preferred_element_type=jnp.float32
            ) * score_scale
            row_top = jnp.max(scores, axis=1, keepdims=True)
            weights = jnp.exp(scores - row_top)
            row_total = jnp.sum(weights, axis=1, keepdims=True)
            mixed = jnp.dot(weights.astype(jnp.bfloat16), kv_ref[asker, 1],
                            preferred_element_type=jnp.float32)
            part_out[asker] = mixed.astype(part_out.dtype)
            stats = jnp.concatenate(
                [row_top, row_total, jnp.zeros((rows, 6), jnp.float32)], axis=1
            )
            stat_out[asker] = stats.T
            part_copy(me, asker).start()
            stat_copy(me, asker).start()

        return carry

    lax.fori_loop(1, count, serve, 0)

    def finish(peer, carry):
        @pl.when(peer < me)
        def _():
            query_copy(me, peer).wait_send()
            part_copy(peer, me).wait_recv()
            stat_copy(peer, me).wait_recv()

        @pl.when(peer > me)
        def _():
            part_copy(me, peer).wait_send()
            stat_copy(me, peer).wait_send()

        return carry

    lax.fori_loop(0, count, finish, 0)


def partials(query_out, kv):
    count, _, rows, _ = kv.shape
    return pl.pallas_call(
        functools.partial(partial_kernel, count),
        out_shape=(
            jax.ShapeDtypeStruct((count, rows, HD), kv.dtype),
            jax.ShapeDtypeStruct((count, 8, rows), jnp.float32),
        ),
        in_specs=[
            pl.BlockSpec(memory_space=pl.ANY),
            pl.BlockSpec(memory_space=pltpu.VMEM),
        ],
        out_specs=(pl.BlockSpec(memory_space=pl.ANY), pl.BlockSpec(memory_space=pl.ANY)),
        scratch_shapes=[
            pltpu.VMEM((count, rows, HD), kv.dtype),
            pltpu.VMEM((count, rows, HD), kv.dtype),
            pltpu.VMEM((count, 8, rows), jnp.float32),
            pltpu.SemaphoreType.DMA((2, count)),
            pltpu.SemaphoreType.DMA((2, count)),
            pltpu.SemaphoreType.DMA((2, count)),
        ],
        compiler_params=pltpu.CompilerParams(
            collective_id=0, has_side_effects=True, vmem_limit_bytes=60 * 1024 * 1024
        ),
    )(query_out, kv)


def attend_kernel(slot_ref, live_ref, q_ref, k_ref, v_ref, first_ref, second_ref,
                  first_stat_ref, second_stat_ref, o_ref):
    head = pl.program_id(0)
    rows = q_ref.shape[0]
    score_scale = HD ** (-0.5)
    dims = (((1,), (1,)), ((), ()))
    raw = lax.dot_general(q_ref[...], k_ref[...], dims, preferred_element_type=jnp.float32)
    row_index = lax.broadcasted_iota(jnp.int32, (rows, rows), 0)
    col_index = lax.broadcasted_iota(jnp.int32, (rows, rows), 1)
    own = jnp.where(row_index >= col_index, raw * score_scale, -jnp.inf)

    def remote(live, part_ref, stat_ref):
        stats = stat_ref[0].T
        top = jnp.where(live, stats[:, 0:1], -jnp.inf)
        total = jnp.where(live, stats[:, 1:2], 0.0)
        part = jnp.where(live, part_ref[0].astype(jnp.float32), 0.0)
        return top, total, part

    first_top, first_total, first_part = remote(live_ref[PICKS * head] > 0, first_ref,
                                                first_stat_ref)
    second_top, second_total, second_part = remote(live_ref[PICKS * head + 1] > 0, second_ref,
                                                   second_stat_ref)
    row_top = jnp.maximum(jnp.maximum(jnp.max(own, axis=1, keepdims=True), first_top),
                          second_top)
    own = jnp.exp(own - row_top)
    first_scale = jnp.exp(first_top - row_top)
    second_scale = jnp.exp(second_top - row_top)
    row_scale = 1.0 / (
        jnp.sum(own, axis=1, keepdims=True) + first_scale * first_total
        + second_scale * second_total
    )
    mixed = jnp.dot((own * row_scale).astype(jnp.bfloat16), v_ref[...],
                    preferred_element_type=jnp.float32)
    mixed += (first_scale * row_scale) * first_part + (second_scale * row_scale) * second_part
    o_ref[...] = mixed.astype(o_ref.dtype)


def attend(slots, live, queries, keys, values, parts, stats):
    rows = queries.shape[0]
    head_block = pl.BlockSpec((rows, HD), lambda h, slot_ref, live_ref: (0, h))

    def picked(j, shape):
        return pl.BlockSpec(
            (1,) + shape, lambda h, slot_ref, live_ref: (slot_ref[PICKS * h + j], 0, 0)
        )

    grid_spec = pltpu.PrefetchScalarGridSpec(
        num_scalar_prefetch=2,
        grid=(HEADS,),
        in_specs=[
            head_block,
            head_block,
            head_block,
            picked(0, (rows, HD)),
            picked(1, (rows, HD)),
            picked(0, (8, rows)),
            picked(1, (8, rows)),
        ],
        out_specs=head_block,
    )
    return pl.pallas_call(
        attend_kernel,
        grid_spec=grid_spec,
        out_shape=jax.ShapeDtypeStruct(queries.shape, queries.dtype),
    )(slots, live, queries, keys, values, parts, parts, stats, stats)


def per_device(queries, keys, values, picks):
    rank_here = lax.axis_index("ctx")
    every_pick = picks[0]
    count = every_pick.shape[0]
    head_ids = lax.broadcasted_iota(jnp.int32, every_pick.shape, 1)
    asked = jnp.sum(jnp.where(every_pick == rank_here, head_ids, 0), axis=(1, 2))
    kv = pack_heads(asked.astype(jnp.int32), keys[0], values[0])
    chosen = lax.dynamic_index_in_dim(every_pick, rank_here, 0, keepdims=False).reshape(-1)
    owners = lax.broadcasted_iota(jnp.int32, (count, HEADS * PICKS), 0)
    wanted = jnp.sum(
        jnp.where(chosen[None, :] == owners, jnp.repeat(lax.iota(jnp.int32, HEADS), PICKS), 0),
        axis=1,
    )
    query_out = pack_heads(wanted.astype(jnp.int32), queries[0])
    parts, stats = partials(query_out, kv)
    live = (chosen >= 0).astype(jnp.int32)
    slots = jnp.maximum(chosen, 0).astype(jnp.int32)
    merged = attend(slots, live, queries[0], keys[0], values[0], parts, stats)
    merged = passed_along(merged[None], "pipe", 1)
    return merged


def solution(mesh):
    placed = (
        P("pipe", "ctx", None),
        P("pipe", "ctx", None),
        P("pipe", "ctx", None),
        P("pipe", None, None, None),
    )
    return jax.shard_map(
        per_device, mesh=mesh, in_specs=placed, out_specs=P("pipe", "ctx", None), check_vma=False
    )
```

```python
import functools

import jax
import jax.numpy as jnp
from jax import lax
from jax.experimental import pallas as pl
from jax.experimental.pallas import tpu as pltpu
from jax.sharding import PartitionSpec as P

HEADS = 16
HD = 128
PICKS = 2
ROUNDS = 4
MESH = pl.DeviceIdType.MESH


def passed_along(value, axis, steps):
    count = lax.axis_size(axis)
    pairs = [(source, (source + steps) % count) for source in range(count)]
    return lax.ppermute(value, axis, pairs)


def pack_kernel(group, count_in, wanted_ref, *refs):
    sources, out_ref = refs[:count_in], refs[count_in]
    base = pl.program_id(0) * group
    for i in range(group):
        column = pl.multiple_of(wanted_ref[base + i] * HD, HD)
        for j, source in enumerate(sources):
            out_ref[i, j] = source[:, pl.ds(column, HD)]


def pack_heads(wanted, *sources):
    count = wanted.shape[0]
    rows, width = sources[0].shape
    group = 8
    whole = pl.BlockSpec((rows, width), lambda g, wanted_ref: (0, 0))
    grid_spec = pltpu.PrefetchScalarGridSpec(
        num_scalar_prefetch=1,
        grid=(count // group,),
        in_specs=[whole] * len(sources),
        out_specs=pl.BlockSpec(
            (group, len(sources), rows, HD), lambda g, wanted_ref: (g, 0, 0, 0)
        ),
    )
    return pl.pallas_call(
        functools.partial(pack_kernel, group, len(sources)),
        grid_spec=grid_spec,
        out_shape=jax.ShapeDtypeStruct((count, len(sources), rows, HD), sources[0].dtype),
    )(wanted, *sources)


def partial_kernel(count, query_out_ref, kv_ref, part_ref, stat_ref, query_in, part_out,
                   stat_out, query_sems, part_sems, stat_sems):
    me = lax.axis_index("ctx")
    rows = part_ref.shape[1]
    score_scale = HD ** (-0.5)
    dims = (((1,), (1,)), ((), ()))
    barrier = pltpu.get_barrier_semaphore()

    def greet(step, carry):
        peer = lax.rem(me + step, count)
        pl.semaphore_signal(barrier, 1, device_id={"ctx": peer}, device_id_type=MESH)
        return carry

    lax.fori_loop(1, count, greet, 0)
    pl.semaphore_wait(barrier, count - 1)

    def query_copy(source, target):
        return pltpu.make_async_remote_copy(
            src_ref=query_out_ref.at[target, 0],
            dst_ref=query_in.at[source],
            send_sem=query_sems.at[0, target],
            recv_sem=query_sems.at[1, source],
            device_id={"ctx": target},
            device_id_type=MESH,
        )

    def part_copy(source, target):
        return pltpu.make_async_remote_copy(
            src_ref=part_out.at[target],
            dst_ref=part_ref.at[source],
            send_sem=part_sems.at[0, target],
            recv_sem=part_sems.at[1, source],
            device_id={"ctx": target},
            device_id_type=MESH,
        )

    def stat_copy(source, target):
        return pltpu.make_async_remote_copy(
            src_ref=stat_out.at[target],
            dst_ref=stat_ref.at[source],
            send_sem=stat_sems.at[0, target],
            recv_sem=stat_sems.at[1, source],
            device_id={"ctx": target},
            device_id_type=MESH,
        )

    def serve(step, carry):
        asker = me + step

        @pl.when(asker < count)
        def _():
            query_copy(asker, me).wait_recv()
            scores = lax.dot_general(
                query_in[asker], kv_ref[asker, 0], dims, preferred_element_type=jnp.float32
            ) * score_scale
            row_top = jnp.max(scores, axis=1, keepdims=True)
            weights = jnp.exp(scores - row_top)
            row_total = jnp.sum(weights, axis=1, keepdims=True)
            mixed = jnp.dot(weights.astype(jnp.bfloat16), kv_ref[asker, 1],
                            preferred_element_type=jnp.float32)
            part_out[asker] = mixed.astype(part_out.dtype)
            stats = jnp.concatenate(
                [row_top, row_total, jnp.zeros((rows, 6), jnp.float32)], axis=1
            )
            stat_out[asker] = stats.T
            part_copy(me, asker).start()
            stat_copy(me, asker).start()

        return carry

    for round_index in range(ROUNDS):
        def ask(i, carry, round_index=round_index):
            owner = i * ROUNDS + round_index

            @pl.when(owner < me)
            def _():
                query_copy(me, owner).start()

            return carry

        def asked(i, carry, round_index=round_index):
            owner = i * ROUNDS + round_index

            @pl.when(owner < me)
            def _():
                query_copy(me, owner).wait_send()

            return carry

        lax.fori_loop(0, count // ROUNDS, ask, 0)
        lax.fori_loop(0, count // ROUNDS, asked, 0)

        @pl.when(lax.rem(me, ROUNDS) == round_index)
        def _():
            lax.fori_loop(1, count, serve, 0)

    def finish(peer, carry):
        @pl.when(peer < me)
        def _():
            part_copy(peer, me).wait_recv()
            stat_copy(peer, me).wait_recv()

        @pl.when(peer > me)
        def _():
            part_copy(me, peer).wait_send()
            stat_copy(me, peer).wait_send()

        return carry

    lax.fori_loop(0, count, finish, 0)


def partials(query_out, kv):
    count, _, rows, _ = kv.shape
    return pl.pallas_call(
        functools.partial(partial_kernel, count),
        out_shape=(
            jax.ShapeDtypeStruct((count, rows, HD), kv.dtype),
            jax.ShapeDtypeStruct((count, 8, rows), jnp.float32),
        ),
        in_specs=[
            pl.BlockSpec(memory_space=pl.ANY),
            pl.BlockSpec(memory_space=pltpu.VMEM),
        ],
        out_specs=(pl.BlockSpec(memory_space=pl.ANY), pl.BlockSpec(memory_space=pl.ANY)),
        scratch_shapes=[
            pltpu.VMEM((count, rows, HD), kv.dtype),
            pltpu.VMEM((count, rows, HD), kv.dtype),
            pltpu.VMEM((count, 8, rows), jnp.float32),
            pltpu.SemaphoreType.DMA((2, count)),
            pltpu.SemaphoreType.DMA((2, count)),
            pltpu.SemaphoreType.DMA((2, count)),
        ],
        compiler_params=pltpu.CompilerParams(
            collective_id=0, has_side_effects=True, vmem_limit_bytes=60 * 1024 * 1024
        ),
    )(query_out, kv)


def attend_kernel(slot_ref, live_ref, q_ref, k_ref, v_ref, first_ref, second_ref,
                  first_stat_ref, second_stat_ref, o_ref):
    head = pl.program_id(0)
    rows = q_ref.shape[0]
    score_scale = HD ** (-0.5)
    dims = (((1,), (1,)), ((), ()))
    raw = lax.dot_general(q_ref[...], k_ref[...], dims, preferred_element_type=jnp.float32)
    row_index = lax.broadcasted_iota(jnp.int32, (rows, rows), 0)
    col_index = lax.broadcasted_iota(jnp.int32, (rows, rows), 1)
    own = jnp.where(row_index >= col_index, raw * score_scale, -jnp.inf)

    def remote(live, part_ref, stat_ref):
        stats = stat_ref[0].T
        top = jnp.where(live, stats[:, 0:1], -jnp.inf)
        total = jnp.where(live, stats[:, 1:2], 0.0)
        part = jnp.where(live, part_ref[0].astype(jnp.float32), 0.0)
        return top, total, part

    first_top, first_total, first_part = remote(live_ref[PICKS * head] > 0, first_ref,
                                                first_stat_ref)
    second_top, second_total, second_part = remote(live_ref[PICKS * head + 1] > 0, second_ref,
                                                   second_stat_ref)
    row_top = jnp.maximum(jnp.maximum(jnp.max(own, axis=1, keepdims=True), first_top),
                          second_top)
    own = jnp.exp(own - row_top)
    first_scale = jnp.exp(first_top - row_top)
    second_scale = jnp.exp(second_top - row_top)
    row_scale = 1.0 / (
        jnp.sum(own, axis=1, keepdims=True) + first_scale * first_total
        + second_scale * second_total
    )
    mixed = jnp.dot((own * row_scale).astype(jnp.bfloat16), v_ref[...],
                    preferred_element_type=jnp.float32)
    mixed += (first_scale * row_scale) * first_part + (second_scale * row_scale) * second_part
    o_ref[...] = mixed.astype(o_ref.dtype)


def attend(slots, live, queries, keys, values, parts, stats):
    rows = queries.shape[0]
    head_block = pl.BlockSpec((rows, HD), lambda h, slot_ref, live_ref: (0, h))

    def picked(j, shape):
        return pl.BlockSpec(
            (1,) + shape, lambda h, slot_ref, live_ref: (slot_ref[PICKS * h + j], 0, 0)
        )

    grid_spec = pltpu.PrefetchScalarGridSpec(
        num_scalar_prefetch=2,
        grid=(HEADS,),
        in_specs=[
            head_block,
            head_block,
            head_block,
            picked(0, (rows, HD)),
            picked(1, (rows, HD)),
            picked(0, (8, rows)),
            picked(1, (8, rows)),
        ],
        out_specs=head_block,
    )
    return pl.pallas_call(
        attend_kernel,
        grid_spec=grid_spec,
        out_shape=jax.ShapeDtypeStruct(queries.shape, queries.dtype),
    )(slots, live, queries, keys, values, parts, parts, stats, stats)


def per_device(queries, keys, values, picks):
    rank_here = lax.axis_index("ctx")
    every_pick = picks[0]
    count = every_pick.shape[0]
    head_ids = lax.broadcasted_iota(jnp.int32, every_pick.shape, 1)
    asked = jnp.sum(jnp.where(every_pick == rank_here, head_ids, 0), axis=(1, 2))
    kv = pack_heads(asked.astype(jnp.int32), keys[0], values[0])
    chosen = lax.dynamic_index_in_dim(every_pick, rank_here, 0, keepdims=False).reshape(-1)
    owners = lax.broadcasted_iota(jnp.int32, (count, HEADS * PICKS), 0)
    wanted = jnp.sum(
        jnp.where(chosen[None, :] == owners, jnp.repeat(lax.iota(jnp.int32, HEADS), PICKS), 0),
        axis=1,
    )
    query_out = pack_heads(wanted.astype(jnp.int32), queries[0])
    parts, stats = partials(query_out, kv)
    live = (chosen >= 0).astype(jnp.int32)
    slots = jnp.maximum(chosen, 0).astype(jnp.int32)
    merged = attend(slots, live, queries[0], keys[0], values[0], parts, stats)
    merged = passed_along(merged[None], "pipe", 1)
    return merged


def solution(mesh):
    placed = (
        P("pipe", "ctx", None),
        P("pipe", "ctx", None),
        P("pipe", "ctx", None),
        P("pipe", None, None, None),
    )
    return jax.shard_map(
        per_device, mesh=mesh, in_specs=placed, out_specs=P("pipe", "ctx", None), check_vma=False
    )
```

```python
import functools

import jax
import jax.numpy as jnp
from jax import lax
from jax.experimental import pallas as pl
from jax.experimental.pallas import tpu as pltpu
from jax.sharding import PartitionSpec as P

HEADS = 16
HD = 128
PICKS = 2
MESH = pl.DeviceIdType.MESH


def passed_along(value, axis, steps):
    count = lax.axis_size(axis)
    pairs = [(source, (source + steps) % count) for source in range(count)]
    return lax.ppermute(value, axis, pairs)


def pack_kernel(group, count_in, wanted_ref, *refs):
    sources, out_ref = refs[:count_in], refs[count_in]
    base = pl.program_id(0) * group
    for i in range(group):
        column = pl.multiple_of(wanted_ref[base + i] * HD, HD)
        for j, source in enumerate(sources):
            out_ref[i, j] = source[:, pl.ds(column, HD)]


def pack_heads(wanted, *sources):
    count = wanted.shape[0]
    rows, width = sources[0].shape
    group = 8
    whole = pl.BlockSpec((rows, width), lambda g, wanted_ref: (0, 0))
    grid_spec = pltpu.PrefetchScalarGridSpec(
        num_scalar_prefetch=1,
        grid=(count // group,),
        in_specs=[whole] * len(sources),
        out_specs=pl.BlockSpec(
            (group, len(sources), rows, HD), lambda g, wanted_ref: (g, 0, 0, 0)
        ),
    )
    return pl.pallas_call(
        functools.partial(pack_kernel, group, len(sources)),
        grid_spec=grid_spec,
        out_shape=jax.ShapeDtypeStruct((count, len(sources), rows, HD), sources[0].dtype),
    )(wanted, *sources)


def split_exact(value):
    high = value.astype(jnp.bfloat16)
    rest = value - high.astype(jnp.float32)
    middle = rest.astype(jnp.bfloat16)
    low = (rest - middle.astype(jnp.float32)).astype(jnp.bfloat16)
    return [high, middle, low]


def partial_kernel(count, query_out_ref, kv_ref, part_ref, query_in, part_out, query_sems,
                   part_sems):
    me = lax.axis_index("ctx")
    rows = query_in.shape[1]
    score_scale = HD ** (-0.5)
    dims = (((1,), (1,)), ((), ()))
    barrier = pltpu.get_barrier_semaphore()

    def greet(step, carry):
        peer = lax.rem(me + step, count)
        pl.semaphore_signal(barrier, 1, device_id={"ctx": peer}, device_id_type=MESH)
        return carry

    lax.fori_loop(1, count, greet, 0)
    pl.semaphore_wait(barrier, count - 1)

    def query_copy(source, target):
        return pltpu.make_async_remote_copy(
            src_ref=query_out_ref.at[target, 0],
            dst_ref=query_in.at[source],
            send_sem=query_sems.at[0, target],
            recv_sem=query_sems.at[1, source],
            device_id={"ctx": target},
            device_id_type=MESH,
        )

    def part_copy(source, target):
        return pltpu.make_async_remote_copy(
            src_ref=part_out.at[target],
            dst_ref=part_ref.at[source],
            send_sem=part_sems.at[0, target],
            recv_sem=part_sems.at[1, source],
            device_id={"ctx": target},
            device_id_type=MESH,
        )

    def ask(step, carry):
        owner = me - step

        @pl.when(owner >= 0)
        def _():
            query_copy(me, owner).start()

        return carry

    lax.fori_loop(1, count, ask, 0)

    def serve(step, carry):
        asker = me + step

        @pl.when(asker < count)
        def _():
            query_copy(asker, me).wait_recv()
            scores = lax.dot_general(
                kv_ref[asker, 0], query_in[asker], dims, preferred_element_type=jnp.float32
            ) * score_scale
            row_top = jnp.max(scores, axis=0, keepdims=True)
            weights = jnp.exp(scores - row_top)
            row_total = jnp.sum(weights, axis=0, keepdims=True)
            mixed = lax.dot_general(
                kv_ref[asker, 1], weights.astype(jnp.bfloat16), (((0,), (0,)), ((), ())),
                preferred_element_type=jnp.float32,
            )
            part_out[asker, :HD, :] = mixed.astype(part_out.dtype)
            pieces = split_exact(row_top) + split_exact(row_total)
            pieces.append(jnp.zeros((16 - len(pieces), rows), jnp.bfloat16))
            part_out[asker, HD:, :] = jnp.concatenate(pieces, axis=0)
            part_copy(me, asker).start()

        return carry

    lax.fori_loop(1, count, serve, 0)

    def finish(peer, carry):
        @pl.when(peer < me)
        def _():
            query_copy(me, peer).wait_send()
            part_copy(peer, me).wait_recv()

        @pl.when(peer > me)
        def _():
            part_copy(me, peer).wait_send()

        return carry

    lax.fori_loop(0, count, finish, 0)


def partials(query_out, kv):
    count, _, rows, _ = kv.shape
    return pl.pallas_call(
        functools.partial(partial_kernel, count),
        out_shape=jax.ShapeDtypeStruct((count, HD + 16, rows), kv.dtype),
        in_specs=[
            pl.BlockSpec(memory_space=pl.ANY),
            pl.BlockSpec(memory_space=pltpu.VMEM),
        ],
        out_specs=pl.BlockSpec(memory_space=pl.ANY),
        scratch_shapes=[
            pltpu.VMEM((count, rows, HD), kv.dtype),
            pltpu.VMEM((count, HD + 16, rows), kv.dtype),
            pltpu.SemaphoreType.DMA((2, count)),
            pltpu.SemaphoreType.DMA((2, count)),
        ],
        compiler_params=pltpu.CompilerParams(
            collective_id=0, has_side_effects=True, vmem_limit_bytes=60 * 1024 * 1024
        ),
    )(query_out, kv)


def attend_kernel(slot_ref, live_ref, q_ref, k_ref, v_ref, first_ref, second_ref, o_ref):
    head = pl.program_id(0)
    rows = q_ref.shape[0]
    score_scale = HD ** (-0.5)
    dims = (((1,), (1,)), ((), ()))
    raw = lax.dot_general(q_ref[...], k_ref[...], dims, preferred_element_type=jnp.float32)
    row_index = lax.broadcasted_iota(jnp.int32, (rows, rows), 0)
    col_index = lax.broadcasted_iota(jnp.int32, (rows, rows), 1)
    own = jnp.where(row_index >= col_index, raw * score_scale, -jnp.inf)

    def remote(live, part_ref):
        slab = part_ref[0]
        coded = slab[HD:, :].astype(jnp.float32)
        top_row = coded[0:1] + coded[1:2] + coded[2:3]
        total_row = coded[3:4] + coded[4:5] + coded[5:6]
        stats = jnp.concatenate([top_row, total_row, coded[6:12]], axis=0).T
        top = jnp.where(live, stats[:, 0:1], -jnp.inf)
        total = jnp.where(live, stats[:, 1:2], 0.0)
        part = jnp.where(live, slab[:HD, :].astype(jnp.float32).T, 0.0)
        return top, total, part

    first_top, first_total, first_part = remote(live_ref[PICKS * head] > 0, first_ref)
    second_top, second_total, second_part = remote(live_ref[PICKS * head + 1] > 0, second_ref)
    row_top = jnp.maximum(jnp.maximum(jnp.max(own, axis=1, keepdims=True), first_top),
                          second_top)
    own = jnp.exp(own - row_top)
    first_scale = jnp.exp(first_top - row_top)
    second_scale = jnp.exp(second_top - row_top)
    row_scale = 1.0 / (
        jnp.sum(own, axis=1, keepdims=True) + first_scale * first_total
        + second_scale * second_total
    )
    mixed = jnp.dot((own * row_scale).astype(jnp.bfloat16), v_ref[...],
                    preferred_element_type=jnp.float32)
    mixed += (first_scale * row_scale) * first_part + (second_scale * row_scale) * second_part
    o_ref[...] = mixed.astype(o_ref.dtype)


def attend(slots, live, queries, keys, values, parts):
    rows = queries.shape[0]
    head_block = pl.BlockSpec((rows, HD), lambda h, slot_ref, live_ref: (0, h))

    def picked(j, shape):
        return pl.BlockSpec(
            (1,) + shape, lambda h, slot_ref, live_ref: (slot_ref[PICKS * h + j], 0, 0)
        )

    grid_spec = pltpu.PrefetchScalarGridSpec(
        num_scalar_prefetch=2,
        grid=(HEADS,),
        in_specs=[
            head_block,
            head_block,
            head_block,
            picked(0, (HD + 16, rows)),
            picked(1, (HD + 16, rows)),
        ],
        out_specs=head_block,
    )
    return pl.pallas_call(
        attend_kernel,
        grid_spec=grid_spec,
        out_shape=jax.ShapeDtypeStruct(queries.shape, queries.dtype),
    )(slots, live, queries, keys, values, parts, parts)


def per_device(queries, keys, values, picks):
    rank_here = lax.axis_index("ctx")
    every_pick = picks[0]
    count = every_pick.shape[0]
    head_ids = lax.broadcasted_iota(jnp.int32, every_pick.shape, 1)
    asked = jnp.sum(jnp.where(every_pick == rank_here, head_ids, 0), axis=(1, 2))
    kv = pack_heads(asked.astype(jnp.int32), keys[0], values[0])
    chosen = lax.dynamic_index_in_dim(every_pick, rank_here, 0, keepdims=False).reshape(-1)
    owners = lax.broadcasted_iota(jnp.int32, (count, HEADS * PICKS), 0)
    wanted = jnp.sum(
        jnp.where(chosen[None, :] == owners, jnp.repeat(lax.iota(jnp.int32, HEADS), PICKS), 0),
        axis=1,
    )
    query_out = pack_heads(wanted.astype(jnp.int32), queries[0])
    parts = partials(query_out, kv)
    live = (chosen >= 0).astype(jnp.int32)
    slots = jnp.maximum(chosen, 0).astype(jnp.int32)
    merged = attend(slots, live, queries[0], keys[0], values[0], parts)
    merged = passed_along(merged[None], "pipe", 1)
    return merged


def solution(mesh):
    placed = (
        P("pipe", "ctx", None),
        P("pipe", "ctx", None),
        P("pipe", "ctx", None),
        P("pipe", None, None, None),
    )
    return jax.shard_map(
        per_device, mesh=mesh, in_specs=placed, out_specs=P("pipe", "ctx", None), check_vma=False
    )
```

```python
import functools

import jax
import jax.numpy as jnp
from jax import lax
from jax.experimental import pallas as pl
from jax.experimental.pallas import tpu as pltpu
from jax.sharding import PartitionSpec as P

HEADS = 16
HD = 128
PICKS = 2
MESH = pl.DeviceIdType.MESH


def passed_along(value, axis, steps):
    count = lax.axis_size(axis)
    pairs = [(source, (source + steps) % count) for source in range(count)]
    return lax.ppermute(value, axis, pairs)


def pack_kernel(group, asked_ref, k_ref, v_ref, out_ref):
    base = pl.program_id(0) * group
    for i in range(group):
        column = pl.multiple_of(asked_ref[base + i] * HD, HD)
        out_ref[i, 0] = k_ref[:, pl.ds(column, HD)]
        out_ref[i, 1] = v_ref[:, pl.ds(column, HD)]


def pack_requested(asked, keys, values):
    count = asked.shape[0]
    rows, width = keys.shape
    group = 8
    whole = pl.BlockSpec((rows, width), lambda g, asked_ref: (0, 0))
    grid_spec = pltpu.PrefetchScalarGridSpec(
        num_scalar_prefetch=1,
        grid=(count // group,),
        in_specs=[whole, whole],
        out_specs=pl.BlockSpec((group, 2, rows, HD), lambda g, asked_ref: (g, 0, 0, 0)),
    )
    return pl.pallas_call(
        functools.partial(pack_kernel, group),
        grid_spec=grid_spec,
        out_shape=jax.ShapeDtypeStruct((count, 2, rows, HD), keys.dtype),
    )(asked, keys, values)


def exchange_kernel(count, send_ref, recv_ref, send_sems, recv_sems):
    me = lax.axis_index("ctx")
    barrier = pltpu.get_barrier_semaphore()

    def greet(step, carry):
        peer = lax.rem(me + step, count)
        pl.semaphore_signal(barrier, 1, device_id={"ctx": peer}, device_id_type=MESH)
        return carry

    lax.fori_loop(1, count, greet, 0)
    pl.semaphore_wait(barrier, count - 1)

    def copy_between(source, target, slot):
        return pltpu.make_async_remote_copy(
            src_ref=send_ref.at[slot],
            dst_ref=recv_ref.at[source],
            send_sem=send_sems.at[slot],
            recv_sem=recv_sems.at[source],
            device_id={"ctx": target},
            device_id_type=MESH,
        )

    def start(step, carry):
        target = me + step

        @pl.when(target < count)
        def _():
            copy_between(me, target, target).start()

        return carry

    lax.fori_loop(1, count, start, 0)

    def finish(peer, carry):
        @pl.when(peer > me)
        def _():
            copy_between(me, peer, peer).wait_send()

        @pl.when(peer < me)
        def _():
            copy_between(peer, peer, peer).wait_recv()

        return carry

    lax.fori_loop(0, count, finish, 0)


def exchange(send):
    count = send.shape[0]
    return pl.pallas_call(
        functools.partial(exchange_kernel, count),
        out_shape=jax.ShapeDtypeStruct(send.shape, send.dtype),
        in_specs=[pl.BlockSpec(memory_space=pl.ANY)],
        out_specs=pl.BlockSpec(memory_space=pl.ANY),
        scratch_shapes=[
            pltpu.SemaphoreType.DMA((count,)),
            pltpu.SemaphoreType.DMA((count,)),
        ],
        compiler_params=pltpu.CompilerParams(collective_id=0, has_side_effects=True),
    )(send)


def attend_kernel(first_head, slot_ref, live_ref, q_ref, k_ref, v_ref, first_ref, second_ref,
                  o_ref):
    head = pl.program_id(0) + first_head
    rows = q_ref.shape[0]
    score_scale = HD ** (-0.5)
    dims = (((1,), (1,)), ((), ()))
    query = q_ref[...]

    def scores_against(key_rows):
        raw = lax.dot_general(query, key_rows, dims, preferred_element_type=jnp.float32)
        return raw * score_scale

    row_index = lax.broadcasted_iota(jnp.int32, (rows, rows), 0)
    col_index = lax.broadcasted_iota(jnp.int32, (rows, rows), 1)
    own = jnp.where(row_index >= col_index, scores_against(k_ref[...]), -jnp.inf)
    live_first = live_ref[PICKS * head] > 0
    live_second = live_ref[PICKS * head + 1] > 0
    first = jnp.where(live_first, scores_against(first_ref[0, 0]), -jnp.inf)
    second = jnp.where(live_second, scores_against(second_ref[0, 0]), -jnp.inf)
    row_top = jnp.maximum(
        jnp.maximum(jnp.max(own, axis=1), jnp.max(first, axis=1)), jnp.max(second, axis=1)
    )[:, None]
    own = jnp.exp(own - row_top)
    first = jnp.exp(first - row_top)
    second = jnp.exp(second - row_top)
    row_scale = 1.0 / (
        jnp.sum(own, axis=1) + jnp.sum(first, axis=1) + jnp.sum(second, axis=1)
    )[:, None]
    first_values = jnp.where(live_first, first_ref[0, 1], jnp.zeros_like(first_ref[0, 1]))
    second_values = jnp.where(live_second, second_ref[0, 1], jnp.zeros_like(second_ref[0, 1]))
    mixed = jnp.dot((own * row_scale).astype(jnp.bfloat16), v_ref[...],
                    preferred_element_type=jnp.float32)
    mixed += jnp.dot((first * row_scale).astype(jnp.bfloat16), first_values,
                     preferred_element_type=jnp.float32)
    mixed += jnp.dot((second * row_scale).astype(jnp.bfloat16), second_values,
                     preferred_element_type=jnp.float32)
    o_ref[...] = mixed.astype(o_ref.dtype)


def attend(first_head, heads, slots, live, queries, keys, values, received):
    rows = queries.shape[0]
    head_block = pl.BlockSpec((rows, HD), lambda h, slot_ref, live_ref: (0, h + first_head))

    def picked(j):
        return pl.BlockSpec(
            (1, 2, rows, HD),
            lambda h, slot_ref, live_ref: (slot_ref[PICKS * (h + first_head) + j], 0, 0, 0),
        )

    grid_spec = pltpu.PrefetchScalarGridSpec(
        num_scalar_prefetch=2,
        grid=(heads,),
        in_specs=[head_block, head_block, head_block, picked(0), picked(1)],
        out_specs=pl.BlockSpec((rows, HD), lambda h, slot_ref, live_ref: (0, h)),
    )
    flops = 4 * heads * rows * 3 * rows * HD
    return pl.pallas_call(
        functools.partial(attend_kernel, first_head),
        grid_spec=grid_spec,
        out_shape=jax.ShapeDtypeStruct((rows, heads * HD), queries.dtype),
        cost_estimate=pl.CostEstimate(
            flops=flops, transcendentals=heads * rows * 3 * rows,
            bytes_accessed=heads * rows * HD * 2 * 8,
        ),
    )(slots, live, queries, keys, values, received, received)


def per_device(queries, keys, values, picks):
    rank_here = lax.axis_index("ctx")
    every_pick = picks[0]
    head_ids = lax.broadcasted_iota(jnp.int32, every_pick.shape, 1)
    asked = jnp.sum(jnp.where(every_pick == rank_here, head_ids, 0), axis=(1, 2))
    send = pack_requested(asked.astype(jnp.int32), keys[0], values[0])
    received = lax.all_to_all(send, "ctx", split_axis=0, concat_axis=0, tiled=True)
    chosen = lax.dynamic_index_in_dim(every_pick, rank_here, 0, keepdims=False).reshape(-1)
    live = (chosen >= 0).astype(jnp.int32)
    slots = jnp.maximum(chosen, 0).astype(jnp.int32)
    groups = 4
    heads = HEADS // groups
    sent = [
        passed_along(
            attend(g * heads, heads, slots, live, queries[0], keys[0], values[0], received)[None],
            "pipe", 1,
        )
        for g in range(groups)
    ]
    return jnp.concatenate(sent, axis=2)


def solution(mesh):
    placed = (
        P("pipe", "ctx", None),
        P("pipe", "ctx", None),
        P("pipe", "ctx", None),
        P("pipe", None, None, None),
    )
    return jax.shard_map(
        per_device, mesh=mesh, in_specs=placed, out_specs=P("pipe", "ctx", None), check_vma=False
    )
```

```python
import functools

import jax
import jax.numpy as jnp
from jax import lax
from jax.experimental import pallas as pl
from jax.experimental.pallas import tpu as pltpu
from jax.sharding import PartitionSpec as P

HEADS = 16
HD = 128
PICKS = 2
MESH = pl.DeviceIdType.MESH


def passed_along(value, axis, steps):
    count = lax.axis_size(axis)
    pairs = [(source, (source + steps) % count) for source in range(count)]
    return lax.ppermute(value, axis, pairs)


def pack_kernel(group, asked_ref, k_ref, v_ref, out_ref):
    base = pl.program_id(0) * group
    for i in range(group):
        column = pl.multiple_of(asked_ref[base + i] * HD, HD)
        out_ref[i, 0] = k_ref[:, pl.ds(column, HD)]
        out_ref[i, 1] = v_ref[:, pl.ds(column, HD)]


def pack_requested(asked, keys, values):
    count = asked.shape[0]
    rows, width = keys.shape
    group = 8
    whole = pl.BlockSpec((rows, width), lambda g, asked_ref: (0, 0))
    grid_spec = pltpu.PrefetchScalarGridSpec(
        num_scalar_prefetch=1,
        grid=(count // group,),
        in_specs=[whole, whole],
        out_specs=pl.BlockSpec((group, 2, rows, HD), lambda g, asked_ref: (g, 0, 0, 0)),
    )
    return pl.pallas_call(
        functools.partial(pack_kernel, group),
        grid_spec=grid_spec,
        out_shape=jax.ShapeDtypeStruct((count, 2, rows, HD), keys.dtype),
    )(asked, keys, values)


def exchange_kernel(count, send_ref, recv_ref, send_sems, recv_sems):
    me = lax.axis_index("ctx")
    barrier = pltpu.get_barrier_semaphore()

    def greet(step, carry):
        peer = lax.rem(me + step, count)
        pl.semaphore_signal(barrier, 1, device_id={"ctx": peer}, device_id_type=MESH)
        return carry

    lax.fori_loop(1, count, greet, 0)
    pl.semaphore_wait(barrier, count - 1)

    def copy_between(source, target, slot):
        return pltpu.make_async_remote_copy(
            src_ref=send_ref.at[slot],
            dst_ref=recv_ref.at[source],
            send_sem=send_sems.at[slot],
            recv_sem=recv_sems.at[source],
            device_id={"ctx": target},
            device_id_type=MESH,
        )

    def start(step, carry):
        target = me + step

        @pl.when(target < count)
        def _():
            copy_between(me, target, target).start()

        return carry

    lax.fori_loop(1, count, start, 0)

    def finish(peer, carry):
        @pl.when(peer > me)
        def _():
            copy_between(me, peer, peer).wait_send()

        @pl.when(peer < me)
        def _():
            copy_between(peer, peer, peer).wait_recv()

        return carry

    lax.fori_loop(0, count, finish, 0)


def exchange(send):
    count = send.shape[0]
    return pl.pallas_call(
        functools.partial(exchange_kernel, count),
        out_shape=jax.ShapeDtypeStruct(send.shape, send.dtype),
        in_specs=[pl.BlockSpec(memory_space=pl.ANY)],
        out_specs=pl.BlockSpec(memory_space=pl.ANY),
        scratch_shapes=[
            pltpu.SemaphoreType.DMA((count,)),
            pltpu.SemaphoreType.DMA((count,)),
        ],
        compiler_params=pltpu.CompilerParams(collective_id=0, has_side_effects=True),
    )(send)


def own_kernel(q_ref, k_ref, v_ref, part_ref, stat_ref):
    rows = q_ref.shape[0]
    score_scale = HD ** (-0.5)
    dims = (((1,), (1,)), ((), ()))
    raw = lax.dot_general(q_ref[...], k_ref[...], dims, preferred_element_type=jnp.float32)
    row_index = lax.broadcasted_iota(jnp.int32, (rows, rows), 0)
    col_index = lax.broadcasted_iota(jnp.int32, (rows, rows), 1)
    own = jnp.where(row_index >= col_index, raw * score_scale, -jnp.inf)
    row_top = jnp.max(own, axis=1, keepdims=True)
    weights = jnp.exp(own - row_top)
    row_total = jnp.sum(weights, axis=1, keepdims=True)
    part_ref[...] = jnp.dot(weights, v_ref[...].astype(jnp.float32),
                            precision=lax.Precision.HIGHEST, preferred_element_type=jnp.float32)
    lane = lax.broadcasted_iota(jnp.int32, (rows, HD), 1)
    stat_ref[...] = jnp.where(lane == 0, row_top, jnp.where(lane == 1, row_total, 0.0))


def own_attention(queries, keys, values):
    rows = queries.shape[0]
    head_block = pl.BlockSpec((rows, HD), lambda h: (0, h))
    return pl.pallas_call(
        own_kernel,
        grid=(HEADS,),
        in_specs=[head_block, head_block, head_block],
        out_specs=(head_block, head_block),
        out_shape=(
            jax.ShapeDtypeStruct(queries.shape, jnp.float32),
            jax.ShapeDtypeStruct(queries.shape, jnp.float32),
        ),
        cost_estimate=pl.CostEstimate(
            flops=4 * HEADS * rows * rows * HD, transcendentals=HEADS * rows * rows,
            bytes_accessed=HEADS * rows * HD * 22,
        ),
    )(queries, keys, values)


def attend_kernel(first_head, slot_ref, live_ref, q_ref, own_part_ref, own_stat_ref, first_ref,
                  second_ref, o_ref):
    head = pl.program_id(0) + first_head
    score_scale = HD ** (-0.5)
    dims = (((1,), (1,)), ((), ()))
    query = q_ref[...]

    def scores_against(key_rows):
        raw = lax.dot_general(query, key_rows, dims, preferred_element_type=jnp.float32)
        return raw * score_scale

    live_first = live_ref[PICKS * head] > 0
    live_second = live_ref[PICKS * head + 1] > 0
    first = jnp.where(live_first, scores_against(first_ref[0, 0]), -jnp.inf)
    second = jnp.where(live_second, scores_against(second_ref[0, 0]), -jnp.inf)
    own_top = own_stat_ref[:, 0:1]
    row_top = jnp.maximum(
        jnp.maximum(own_top, jnp.max(first, axis=1, keepdims=True)),
        jnp.max(second, axis=1, keepdims=True),
    )
    own_scale = jnp.exp(own_top - row_top)
    first = jnp.exp(first - row_top)
    second = jnp.exp(second - row_top)
    row_scale = 1.0 / (
        own_scale * own_stat_ref[:, 1:2] + jnp.sum(first, axis=1, keepdims=True)
        + jnp.sum(second, axis=1, keepdims=True)
    )
    first_values = jnp.where(live_first, first_ref[0, 1], jnp.zeros_like(first_ref[0, 1]))
    second_values = jnp.where(live_second, second_ref[0, 1], jnp.zeros_like(second_ref[0, 1]))
    mixed = (own_scale * row_scale) * own_part_ref[...]
    mixed += jnp.dot((first * row_scale).astype(jnp.bfloat16), first_values,
                     preferred_element_type=jnp.float32)
    mixed += jnp.dot((second * row_scale).astype(jnp.bfloat16), second_values,
                     preferred_element_type=jnp.float32)
    o_ref[...] = mixed.astype(o_ref.dtype)


def attend(first_head, heads, slots, live, queries, own_part, own_stat, received):
    rows = queries.shape[0]
    head_block = pl.BlockSpec((rows, HD), lambda h, slot_ref, live_ref: (0, h + first_head))

    def picked(j):
        return pl.BlockSpec(
            (1, 2, rows, HD),
            lambda h, slot_ref, live_ref: (slot_ref[PICKS * (h + first_head) + j], 0, 0, 0),
        )

    grid_spec = pltpu.PrefetchScalarGridSpec(
        num_scalar_prefetch=2,
        grid=(heads,),
        in_specs=[head_block, head_block, head_block, picked(0), picked(1)],
        out_specs=pl.BlockSpec((rows, HD), lambda h, slot_ref, live_ref: (0, h)),
    )
    flops = 4 * heads * rows * 2 * rows * HD
    return pl.pallas_call(
        functools.partial(attend_kernel, first_head),
        grid_spec=grid_spec,
        out_shape=jax.ShapeDtypeStruct((rows, heads * HD), queries.dtype),
        cost_estimate=pl.CostEstimate(
            flops=flops, transcendentals=heads * rows * 2 * rows,
            bytes_accessed=heads * rows * HD * 2 * 8,
        ),
    )(slots, live, queries, own_part, own_stat, received, received)


def per_device(queries, keys, values, picks):
    rank_here = lax.axis_index("ctx")
    every_pick = picks[0]
    head_ids = lax.broadcasted_iota(jnp.int32, every_pick.shape, 1)
    asked = jnp.sum(jnp.where(every_pick == rank_here, head_ids, 0), axis=(1, 2))
    send = pack_requested(asked.astype(jnp.int32), keys[0], values[0])
    received = lax.all_to_all(send, "ctx", split_axis=0, concat_axis=0, tiled=True)
    chosen = lax.dynamic_index_in_dim(every_pick, rank_here, 0, keepdims=False).reshape(-1)
    live = (chosen >= 0).astype(jnp.int32)
    slots = jnp.maximum(chosen, 0).astype(jnp.int32)
    own_part, own_stat = own_attention(queries[0], keys[0], values[0])
    groups = 4
    heads = HEADS // groups
    sent = [
        passed_along(
            attend(g * heads, heads, slots, live, queries[0], own_part, own_stat, received)[None],
            "pipe", 1,
        )
        for g in range(groups)
    ]
    return jnp.concatenate(sent, axis=2)


def solution(mesh):
    placed = (
        P("pipe", "ctx", None),
        P("pipe", "ctx", None),
        P("pipe", "ctx", None),
        P("pipe", None, None, None),
    )
    return jax.shard_map(
        per_device, mesh=mesh, in_specs=placed, out_specs=P("pipe", "ctx", None), check_vma=False
    )
```

```python
import functools

import jax
import jax.numpy as jnp
from jax import lax
from jax.experimental import pallas as pl
from jax.experimental.pallas import tpu as pltpu
from jax.sharding import PartitionSpec as P

HEADS = 16
HD = 128
PICKS = 2
MESH = pl.DeviceIdType.MESH


def passed_along(value, axis, steps):
    count = lax.axis_size(axis)
    pairs = [(source, (source + steps) % count) for source in range(count)]
    return lax.ppermute(value, axis, pairs)


def pack_kernel(group, asked_ref, k_ref, v_ref, out_ref):
    base = pl.program_id(0) * group
    for i in range(group):
        column = pl.multiple_of(asked_ref[base + i] * HD, HD)
        out_ref[i, 0] = k_ref[:, pl.ds(column, HD)]
        out_ref[i, 1] = v_ref[:, pl.ds(column, HD)]


def pack_requested(asked, keys, values):
    count = asked.shape[0]
    rows, width = keys.shape
    group = 8
    whole = pl.BlockSpec((rows, width), lambda g, asked_ref: (0, 0))
    grid_spec = pltpu.PrefetchScalarGridSpec(
        num_scalar_prefetch=1,
        grid=(count // group,),
        in_specs=[whole, whole],
        out_specs=pl.BlockSpec((group, 2, rows, HD), lambda g, asked_ref: (g, 0, 0, 0)),
    )
    return pl.pallas_call(
        functools.partial(pack_kernel, group),
        grid_spec=grid_spec,
        out_shape=jax.ShapeDtypeStruct((count, 2, rows, HD), keys.dtype),
    )(asked, keys, values)


def exchange_kernel(count, send_ref, recv_ref, send_sems, recv_sems):
    me = lax.axis_index("ctx")
    barrier = pltpu.get_barrier_semaphore()

    def greet(step, carry):
        peer = lax.rem(me + step, count)
        pl.semaphore_signal(barrier, 1, device_id={"ctx": peer}, device_id_type=MESH)
        return carry

    lax.fori_loop(1, count, greet, 0)
    pl.semaphore_wait(barrier, count - 1)

    def copy_between(source, target, slot):
        return pltpu.make_async_remote_copy(
            src_ref=send_ref.at[slot],
            dst_ref=recv_ref.at[source],
            send_sem=send_sems.at[slot],
            recv_sem=recv_sems.at[source],
            device_id={"ctx": target},
            device_id_type=MESH,
        )

    def start(step, carry):
        target = me + step

        @pl.when(target < count)
        def _():
            copy_between(me, target, target).start()

        return carry

    lax.fori_loop(1, count, start, 0)

    def finish(peer, carry):
        @pl.when(peer > me)
        def _():
            copy_between(me, peer, peer).wait_send()

        @pl.when(peer < me)
        def _():
            copy_between(peer, peer, peer).wait_recv()

        return carry

    lax.fori_loop(0, count, finish, 0)


def exchange(send):
    count = send.shape[0]
    return pl.pallas_call(
        functools.partial(exchange_kernel, count),
        out_shape=jax.ShapeDtypeStruct(send.shape, send.dtype),
        in_specs=[pl.BlockSpec(memory_space=pl.ANY)],
        out_specs=pl.BlockSpec(memory_space=pl.ANY),
        scratch_shapes=[
            pltpu.SemaphoreType.DMA((count,)),
            pltpu.SemaphoreType.DMA((count,)),
        ],
        compiler_params=pltpu.CompilerParams(collective_id=0, has_side_effects=True),
    )(send)


def attend_kernel(first_head, slot_ref, live_ref, q_ref, k_ref, v_ref, first_ref, second_ref,
                  o_ref):
    head = pl.program_id(0) + first_head
    rows = q_ref.shape[0]
    score_scale = HD ** (-0.5)
    dims = (((1,), (1,)), ((), ()))
    query = q_ref[...]

    def scores_against(key_rows):
        raw = lax.dot_general(query, key_rows, dims, preferred_element_type=jnp.float32)
        return raw * score_scale

    row_index = lax.broadcasted_iota(jnp.int32, (rows, rows), 0)
    col_index = lax.broadcasted_iota(jnp.int32, (rows, rows), 1)
    own = jnp.where(row_index >= col_index, scores_against(k_ref[...]), -jnp.inf)
    first_bias = jnp.where(live_ref[PICKS * head] > 0, 0.0, -jnp.inf)
    second_bias = jnp.where(live_ref[PICKS * head + 1] > 0, 0.0, -jnp.inf)
    first = scores_against(first_ref[0, 0]) + first_bias
    second = scores_against(second_ref[0, 0]) + second_bias
    row_top = jnp.maximum(
        jnp.maximum(jnp.max(own, axis=1), jnp.max(first, axis=1)), jnp.max(second, axis=1)
    )[:, None]
    own = jnp.exp(own - row_top)
    first = jnp.exp(first - row_top)
    second = jnp.exp(second - row_top)
    row_scale = 1.0 / (
        jnp.sum(own, axis=1) + jnp.sum(first, axis=1) + jnp.sum(second, axis=1)
    )[:, None]
    mixed = jnp.dot((own * row_scale).astype(jnp.bfloat16), v_ref[...],
                    preferred_element_type=jnp.float32)
    mixed += jnp.dot((first * row_scale).astype(jnp.bfloat16), first_ref[0, 1],
                     preferred_element_type=jnp.float32)
    mixed += jnp.dot((second * row_scale).astype(jnp.bfloat16), second_ref[0, 1],
                     preferred_element_type=jnp.float32)
    o_ref[...] = mixed.astype(o_ref.dtype)


def attend(first_head, heads, slots, live, queries, keys, values, received):
    rows = queries.shape[0]
    head_block = pl.BlockSpec((rows, HD), lambda h, slot_ref, live_ref: (0, h + first_head))

    def picked(j):
        return pl.BlockSpec(
            (1, 2, rows, HD),
            lambda h, slot_ref, live_ref: (slot_ref[PICKS * (h + first_head) + j], 0, 0, 0),
        )

    grid_spec = pltpu.PrefetchScalarGridSpec(
        num_scalar_prefetch=2,
        grid=(heads,),
        in_specs=[head_block, head_block, head_block, picked(0), picked(1)],
        out_specs=pl.BlockSpec((rows, HD), lambda h, slot_ref, live_ref: (0, h)),
    )
    flops = 4 * heads * rows * 3 * rows * HD
    return pl.pallas_call(
        functools.partial(attend_kernel, first_head),
        grid_spec=grid_spec,
        out_shape=jax.ShapeDtypeStruct((rows, heads * HD), queries.dtype),
        cost_estimate=pl.CostEstimate(
            flops=flops, transcendentals=heads * rows * 3 * rows,
            bytes_accessed=heads * rows * HD * 2 * 8,
        ),
    )(slots, live, queries, keys, values, received, received)


def per_device(queries, keys, values, picks):
    rank_here = lax.axis_index("ctx")
    every_pick = picks[0]
    head_ids = lax.broadcasted_iota(jnp.int32, every_pick.shape, 1)
    asked = jnp.sum(jnp.where(every_pick == rank_here, head_ids, 0), axis=(1, 2))
    send = pack_requested(asked.astype(jnp.int32), keys[0], values[0])
    received = lax.all_to_all(send, "ctx", split_axis=0, concat_axis=0, tiled=True)
    chosen = lax.dynamic_index_in_dim(every_pick, rank_here, 0, keepdims=False).reshape(-1)
    live = (chosen >= 0).astype(jnp.int32)
    slots = jnp.maximum(chosen, 0).astype(jnp.int32)
    sizes = (2, 4, 4, 4, 2)
    starts = [sum(sizes[:g]) for g in range(len(sizes))]
    sent = [
        passed_along(
            attend(first, heads, slots, live, queries[0], keys[0], values[0], received)[None],
            "pipe", 1,
        )
        for first, heads in zip(starts, sizes)
    ]
    return jnp.concatenate(sent, axis=2)


def solution(mesh):
    placed = (
        P("pipe", "ctx", None),
        P("pipe", "ctx", None),
        P("pipe", "ctx", None),
        P("pipe", None, None, None),
    )
    return jax.shard_map(
        per_device, mesh=mesh, in_specs=placed, out_specs=P("pipe", "ctx", None), check_vma=False
    )
```

```python
import functools

import jax
import jax.numpy as jnp
from jax import lax
from jax.experimental import pallas as pl
from jax.experimental.pallas import tpu as pltpu
from jax.sharding import PartitionSpec as P

HEADS = 16
HD = 128
PICKS = 2
MESH = pl.DeviceIdType.MESH


def passed_along(value, axis, steps):
    count = lax.axis_size(axis)
    pairs = [(source, (source + steps) % count) for source in range(count)]
    return lax.ppermute(value, axis, pairs)


def pack_kernel(group, asked_ref, k_ref, v_ref, out_ref):
    base = pl.program_id(0) * group
    for i in range(group):
        column = pl.multiple_of(asked_ref[base + i] * HD, HD)
        out_ref[i, 0] = k_ref[:, pl.ds(column, HD)]
        out_ref[i, 1] = v_ref[:, pl.ds(column, HD)]


def pack_requested(asked, keys, values):
    count = asked.shape[0]
    rows, width = keys.shape
    group = 8
    whole = pl.BlockSpec((rows, width), lambda g, asked_ref: (0, 0))
    grid_spec = pltpu.PrefetchScalarGridSpec(
        num_scalar_prefetch=1,
        grid=(count // group,),
        in_specs=[whole, whole],
        out_specs=pl.BlockSpec((group, 2, rows, HD), lambda g, asked_ref: (g, 0, 0, 0)),
    )
    return pl.pallas_call(
        functools.partial(pack_kernel, group),
        grid_spec=grid_spec,
        out_shape=jax.ShapeDtypeStruct((count, 2, rows, HD), keys.dtype),
    )(asked, keys, values)


def exchange_kernel(count, send_ref, recv_ref, send_sems, recv_sems):
    me = lax.axis_index("ctx")
    barrier = pltpu.get_barrier_semaphore()

    def greet(step, carry):
        peer = lax.rem(me + step, count)
        pl.semaphore_signal(barrier, 1, device_id={"ctx": peer}, device_id_type=MESH)
        return carry

    lax.fori_loop(1, count, greet, 0)
    pl.semaphore_wait(barrier, count - 1)

    def copy_between(source, target, slot):
        return pltpu.make_async_remote_copy(
            src_ref=send_ref.at[slot],
            dst_ref=recv_ref.at[source],
            send_sem=send_sems.at[slot],
            recv_sem=recv_sems.at[source],
            device_id={"ctx": target},
            device_id_type=MESH,
        )

    def start(step, carry):
        target = me + step

        @pl.when(target < count)
        def _():
            copy_between(me, target, target).start()

        return carry

    lax.fori_loop(1, count, start, 0)

    def finish(peer, carry):
        @pl.when(peer > me)
        def _():
            copy_between(me, peer, peer).wait_send()

        @pl.when(peer < me)
        def _():
            copy_between(peer, peer, peer).wait_recv()

        return carry

    lax.fori_loop(0, count, finish, 0)


def exchange(send):
    count = send.shape[0]
    return pl.pallas_call(
        functools.partial(exchange_kernel, count),
        out_shape=jax.ShapeDtypeStruct(send.shape, send.dtype),
        in_specs=[pl.BlockSpec(memory_space=pl.ANY)],
        out_specs=pl.BlockSpec(memory_space=pl.ANY),
        scratch_shapes=[
            pltpu.SemaphoreType.DMA((count,)),
            pltpu.SemaphoreType.DMA((count,)),
        ],
        compiler_params=pltpu.CompilerParams(collective_id=0, has_side_effects=True),
    )(send)


def attend_kernel(live_ref, q_ref, k_ref, v_ref, picked_ref, o_ref, out_buf, sems):
    head = pl.program_id(0)
    heads = pl.num_programs(0)
    rows = q_ref.shape[0]
    pipe_size = lax.axis_size("pipe")
    here = lax.axis_index("pipe")
    after = lax.rem(here + 1, pipe_size)
    before = lax.rem(here + pipe_size - 1, pipe_size)

    @pl.when(head == 0)
    def _():
        barrier = pltpu.get_barrier_semaphore()
        for peer in (before, after):
            pl.semaphore_signal(barrier, 1, device_id={"pipe": peer}, device_id_type=MESH)
        pl.semaphore_wait(barrier, 2)

    score_scale = HD ** (-0.5)
    dims = (((1,), (1,)), ((), ()))
    query = q_ref[...]

    def scores_against(key_rows):
        raw = lax.dot_general(query, key_rows, dims, preferred_element_type=jnp.float32)
        return raw * score_scale

    row_index = lax.broadcasted_iota(jnp.int32, (rows, rows), 0)
    col_index = lax.broadcasted_iota(jnp.int32, (rows, rows), 1)
    own = jnp.where(row_index >= col_index, scores_against(k_ref[...]), -jnp.inf)
    first_bias = jnp.where(live_ref[PICKS * head] > 0, 0.0, -jnp.inf)
    second_bias = jnp.where(live_ref[PICKS * head + 1] > 0, 0.0, -jnp.inf)
    first = scores_against(picked_ref[0, 0]) + first_bias
    second = scores_against(picked_ref[1, 0]) + second_bias
    row_top = jnp.maximum(
        jnp.maximum(jnp.max(own, axis=1), jnp.max(first, axis=1)), jnp.max(second, axis=1)
    )[:, None]
    own = jnp.exp(own - row_top)
    first = jnp.exp(first - row_top)
    second = jnp.exp(second - row_top)
    row_scale = 1.0 / (
        jnp.sum(own, axis=1) + jnp.sum(first, axis=1) + jnp.sum(second, axis=1)
    )[:, None]
    mixed = jnp.dot((own * row_scale).astype(jnp.bfloat16), v_ref[...],
                    preferred_element_type=jnp.float32)
    mixed += jnp.dot((first * row_scale).astype(jnp.bfloat16), picked_ref[0, 1],
                     preferred_element_type=jnp.float32)
    mixed += jnp.dot((second * row_scale).astype(jnp.bfloat16), picked_ref[1, 1],
                     preferred_element_type=jnp.float32)
    out_buf[head] = mixed.astype(out_buf.dtype)

    def relay(slot):
        return pltpu.make_async_remote_copy(
            src_ref=out_buf.at[slot],
            dst_ref=o_ref.at[:, pl.ds(pl.multiple_of(slot * HD, HD), HD)],
            send_sem=sems.at[0, slot],
            recv_sem=sems.at[1, slot],
            device_id={"pipe": after},
            device_id_type=MESH,
        )

    relay(head).start()

    @pl.when(head == heads - 1)
    def _():
        def finish(slot, carry):
            relay(slot).wait_send()
            relay(slot).wait_recv()
            return carry

        lax.fori_loop(0, heads, finish, 0)


def attend_and_pass(live, queries, keys, values, picked):
    rows = queries.shape[0]
    head_block = pl.BlockSpec((rows, HD), lambda h, live_ref: (0, h))
    grid_spec = pltpu.PrefetchScalarGridSpec(
        num_scalar_prefetch=1,
        grid=(HEADS,),
        in_specs=[
            head_block,
            head_block,
            head_block,
            pl.BlockSpec((PICKS, 2, rows, HD), lambda h, live_ref: (h, 0, 0, 0)),
        ],
        out_specs=pl.BlockSpec(memory_space=pl.ANY),
        scratch_shapes=[
            pltpu.VMEM((HEADS, rows, HD), queries.dtype),
            pltpu.SemaphoreType.DMA((2, HEADS)),
        ],
    )
    return pl.pallas_call(
        attend_kernel,
        grid_spec=grid_spec,
        out_shape=jax.ShapeDtypeStruct(queries.shape, queries.dtype),
        compiler_params=pltpu.CompilerParams(collective_id=0, has_side_effects=True),
    )(live, queries, keys, values, picked)


def per_device(queries, keys, values, picks):
    rank_here = lax.axis_index("ctx")
    every_pick = picks[0]
    head_ids = lax.broadcasted_iota(jnp.int32, every_pick.shape, 1)
    asked = jnp.sum(jnp.where(every_pick == rank_here, head_ids, 0), axis=(1, 2))
    send = pack_requested(asked.astype(jnp.int32), keys[0], values[0])
    received = lax.all_to_all(send, "ctx", split_axis=0, concat_axis=0, tiled=True)
    chosen = lax.dynamic_index_in_dim(every_pick, rank_here, 0, keepdims=False).reshape(-1)
    live = (chosen >= 0).astype(jnp.int32)
    slots = jnp.maximum(chosen, 0).astype(jnp.int32)
    picked = jnp.take(received, slots, axis=0)
    merged = attend_and_pass(live, queries[0], keys[0], values[0], picked)
    return merged[None]


def solution(mesh):
    placed = (
        P("pipe", "ctx", None),
        P("pipe", "ctx", None),
        P("pipe", "ctx", None),
        P("pipe", None, None, None),
    )
    return jax.shard_map(
        per_device, mesh=mesh, in_specs=placed, out_specs=P("pipe", "ctx", None), check_vma=False
    )
```

```python
import functools

import jax
import jax.numpy as jnp
from jax import lax
from jax.experimental import pallas as pl
from jax.experimental.pallas import tpu as pltpu
from jax.sharding import PartitionSpec as P

HEADS = 16
HD = 128
PICKS = 2
MESH = pl.DeviceIdType.MESH


def passed_along(value, axis, steps):
    count = lax.axis_size(axis)
    pairs = [(source, (source + steps) % count) for source in range(count)]
    return lax.ppermute(value, axis, pairs)


def pack_kernel(group, asked_ref, k_ref, v_ref, out_ref):
    base = pl.program_id(0) * group
    for i in range(group):
        column = pl.multiple_of(asked_ref[base + i] * HD, HD)
        out_ref[i, 0] = k_ref[:, pl.ds(column, HD)]
        out_ref[i, 1] = v_ref[:, pl.ds(column, HD)]


def pack_requested(asked, keys, values):
    count = asked.shape[0]
    rows, width = keys.shape
    group = 8
    whole = pl.BlockSpec((rows, width), lambda g, asked_ref: (0, 0))
    grid_spec = pltpu.PrefetchScalarGridSpec(
        num_scalar_prefetch=1,
        grid=(count // group,),
        in_specs=[whole, whole],
        out_specs=pl.BlockSpec((group, 2, rows, HD), lambda g, asked_ref: (g, 0, 0, 0)),
    )
    return pl.pallas_call(
        functools.partial(pack_kernel, group),
        grid_spec=grid_spec,
        out_shape=jax.ShapeDtypeStruct((count, 2, rows, HD), keys.dtype),
    )(asked, keys, values)


def exchange_kernel(count, send_ref, recv_ref, send_sems, recv_sems):
    me = lax.axis_index("ctx")
    barrier = pltpu.get_barrier_semaphore()

    def greet(step, carry):
        peer = lax.rem(me + step, count)
        pl.semaphore_signal(barrier, 1, device_id={"ctx": peer}, device_id_type=MESH)
        return carry

    lax.fori_loop(1, count, greet, 0)
    pl.semaphore_wait(barrier, count - 1)

    def copy_between(source, target, slot):
        return pltpu.make_async_remote_copy(
            src_ref=send_ref.at[slot],
            dst_ref=recv_ref.at[source],
            send_sem=send_sems.at[slot],
            recv_sem=recv_sems.at[source],
            device_id={"ctx": target},
            device_id_type=MESH,
        )

    def start(step, carry):
        target = me + step

        @pl.when(target < count)
        def _():
            copy_between(me, target, target).start()

        return carry

    lax.fori_loop(1, count, start, 0)

    def finish(peer, carry):
        @pl.when(peer > me)
        def _():
            copy_between(me, peer, peer).wait_send()

        @pl.when(peer < me)
        def _():
            copy_between(peer, peer, peer).wait_recv()

        return carry

    lax.fori_loop(0, count, finish, 0)


def exchange(send):
    count = send.shape[0]
    return pl.pallas_call(
        functools.partial(exchange_kernel, count),
        out_shape=jax.ShapeDtypeStruct(send.shape, send.dtype),
        in_specs=[pl.BlockSpec(memory_space=pl.ANY)],
        out_specs=pl.BlockSpec(memory_space=pl.ANY),
        scratch_shapes=[
            pltpu.SemaphoreType.DMA((count,)),
            pltpu.SemaphoreType.DMA((count,)),
        ],
        compiler_params=pltpu.CompilerParams(collective_id=0, has_side_effects=True),
    )(send)


def attend_kernel(live_ref, q_ref, k_ref, v_ref, picked_ref, o_ref, out_buf, sems):
    head = pl.program_id(0)
    heads = pl.num_programs(0)
    rows = q_ref.shape[0]
    pipe_size = lax.axis_size("pipe")
    here = lax.axis_index("pipe")
    after = lax.rem(here + 1, pipe_size)
    before = lax.rem(here + pipe_size - 1, pipe_size)

    @pl.when(head == 0)
    def _():
        barrier = pltpu.get_barrier_semaphore()
        for peer in (before, after):
            pl.semaphore_signal(barrier, 1, device_id={"pipe": peer}, device_id_type=MESH)
        pl.semaphore_wait(barrier, 2)

    score_scale = HD ** (-0.5)
    dims = (((1,), (1,)), ((), ()))
    query = q_ref[...]

    def scores_against(key_rows):
        raw = lax.dot_general(query, key_rows, dims, preferred_element_type=jnp.float32)
        return raw * score_scale

    row_index = lax.broadcasted_iota(jnp.int32, (rows, rows), 0)
    col_index = lax.broadcasted_iota(jnp.int32, (rows, rows), 1)
    own = jnp.where(row_index >= col_index, scores_against(k_ref[...]), -jnp.inf)
    first_bias = jnp.where(live_ref[PICKS * head] > 0, 0.0, -jnp.inf)
    second_bias = jnp.where(live_ref[PICKS * head + 1] > 0, 0.0, -jnp.inf)
    first = scores_against(picked_ref[0, 0]) + first_bias
    second = scores_against(picked_ref[1, 0]) + second_bias
    row_top = jnp.maximum(
        jnp.maximum(jnp.max(own, axis=1), jnp.max(first, axis=1)), jnp.max(second, axis=1)
    )[:, None]
    own = jnp.exp(own - row_top)
    first = jnp.exp(first - row_top)
    second = jnp.exp(second - row_top)
    row_scale = 1.0 / (
        jnp.sum(own, axis=1) + jnp.sum(first, axis=1) + jnp.sum(second, axis=1)
    )[:, None]
    mixed = jnp.dot((own * row_scale).astype(jnp.bfloat16), v_ref[...],
                    preferred_element_type=jnp.float32)
    mixed += jnp.dot((first * row_scale).astype(jnp.bfloat16), picked_ref[0, 1],
                     preferred_element_type=jnp.float32)
    mixed += jnp.dot((second * row_scale).astype(jnp.bfloat16), picked_ref[1, 1],
                     preferred_element_type=jnp.float32)
    out_buf[head] = mixed.astype(out_buf.dtype)

    def relay(slot):
        return pltpu.make_async_remote_copy(
            src_ref=out_buf.at[slot],
            dst_ref=o_ref.at[:, pl.ds(pl.multiple_of(slot * HD, HD), HD)],
            send_sem=sems.at[0, slot],
            recv_sem=sems.at[1, slot],
            device_id={"pipe": after},
            device_id_type=MESH,
        )

    relay(head).start()

    @pl.when(head == heads - 1)
    def _():
        def finish(slot, carry):
            relay(slot).wait_send()
            relay(slot).wait_recv()
            return carry

        lax.fori_loop(0, heads, finish, 0)


def attend_and_pass(live, queries, keys, values, picked):
    rows = queries.shape[0]
    head_block = pl.BlockSpec((rows, HD), lambda h, live_ref: (0, h))
    grid_spec = pltpu.PrefetchScalarGridSpec(
        num_scalar_prefetch=1,
        grid=(HEADS,),
        in_specs=[
            head_block,
            head_block,
            head_block,
            pl.BlockSpec((PICKS, 2, rows, HD), lambda h, live_ref: (h, 0, 0, 0)),
        ],
        out_specs=pl.BlockSpec(memory_space=pl.ANY),
        scratch_shapes=[
            pltpu.VMEM((HEADS, rows, HD), queries.dtype),
            pltpu.SemaphoreType.DMA((2, HEADS)),
        ],
    )
    return pl.pallas_call(
        attend_kernel,
        grid_spec=grid_spec,
        out_shape=jax.ShapeDtypeStruct(queries.shape, queries.dtype),
        compiler_params=pltpu.CompilerParams(collective_id=0, has_side_effects=True),
    )(live, queries, keys, values, picked)


def gather_kernel(slot_ref, source_ref, out_ref):
    out_ref[...] = source_ref[...]


def gather_slots(slots, received):
    count = slots.shape[0]
    block = (1,) + received.shape[1:]
    grid_spec = pltpu.PrefetchScalarGridSpec(
        num_scalar_prefetch=1,
        grid=(count,),
        in_specs=[pl.BlockSpec(block, lambda i, slot_ref: (slot_ref[i], 0, 0, 0))],
        out_specs=pl.BlockSpec(block, lambda i, slot_ref: (i, 0, 0, 0)),
    )
    return pl.pallas_call(
        gather_kernel,
        grid_spec=grid_spec,
        out_shape=jax.ShapeDtypeStruct((count,) + received.shape[1:], received.dtype),
    )(slots, received)


def per_device(queries, keys, values, picks):
    rank_here = lax.axis_index("ctx")
    every_pick = picks[0]
    head_ids = lax.broadcasted_iota(jnp.int32, every_pick.shape, 1)
    asked = jnp.sum(jnp.where(every_pick == rank_here, head_ids, 0), axis=(1, 2))
    send = pack_requested(asked.astype(jnp.int32), keys[0], values[0])
    received = lax.all_to_all(send, "ctx", split_axis=0, concat_axis=0, tiled=True)
    chosen = lax.dynamic_index_in_dim(every_pick, rank_here, 0, keepdims=False).reshape(-1)
    live = (chosen >= 0).astype(jnp.int32)
    slots = jnp.maximum(chosen, 0).astype(jnp.int32)
    picked = gather_slots(slots, received)
    merged = attend_and_pass(live, queries[0], keys[0], values[0], picked)
    return merged[None]


def solution(mesh):
    placed = (
        P("pipe", "ctx", None),
        P("pipe", "ctx", None),
        P("pipe", "ctx", None),
        P("pipe", None, None, None),
    )
    return jax.shard_map(
        per_device, mesh=mesh, in_specs=placed, out_specs=P("pipe", "ctx", None), check_vma=False
    )
```

```python
import functools

import jax
import jax.numpy as jnp
from jax import lax
from jax.experimental import pallas as pl
from jax.experimental.pallas import tpu as pltpu
from jax.sharding import PartitionSpec as P

HEADS = 16
HD = 128
PICKS = 2
MESH = pl.DeviceIdType.MESH


def passed_along(value, axis, steps):
    count = lax.axis_size(axis)
    pairs = [(source, (source + steps) % count) for source in range(count)]
    return lax.ppermute(value, axis, pairs)


def pack_kernel(group, asked_ref, k_ref, v_ref, out_ref):
    base = pl.program_id(0) * group
    for i in range(group):
        column = pl.multiple_of(asked_ref[base + i] * HD, HD)
        out_ref[i, 0] = k_ref[:, pl.ds(column, HD)]
        out_ref[i, 1] = v_ref[:, pl.ds(column, HD)]


def pack_requested(asked, keys, values):
    count = asked.shape[0]
    rows, width = keys.shape
    group = 8
    whole = pl.BlockSpec((rows, width), lambda g, asked_ref: (0, 0))
    grid_spec = pltpu.PrefetchScalarGridSpec(
        num_scalar_prefetch=1,
        grid=(count // group,),
        in_specs=[whole, whole],
        out_specs=pl.BlockSpec((group, 2, rows, HD), lambda g, asked_ref: (g, 0, 0, 0)),
    )
    return pl.pallas_call(
        functools.partial(pack_kernel, group),
        grid_spec=grid_spec,
        out_shape=jax.ShapeDtypeStruct((count, 2, rows, HD), keys.dtype),
    )(asked, keys, values)


def exchange_kernel(count, send_ref, recv_ref, send_sems, recv_sems):
    me = lax.axis_index("ctx")
    barrier = pltpu.get_barrier_semaphore()

    def greet(step, carry):
        peer = lax.rem(me + step, count)
        pl.semaphore_signal(barrier, 1, device_id={"ctx": peer}, device_id_type=MESH)
        return carry

    lax.fori_loop(1, count, greet, 0)
    pl.semaphore_wait(barrier, count - 1)

    def copy_between(source, target, slot):
        return pltpu.make_async_remote_copy(
            src_ref=send_ref.at[slot],
            dst_ref=recv_ref.at[source],
            send_sem=send_sems.at[slot],
            recv_sem=recv_sems.at[source],
            device_id={"ctx": target},
            device_id_type=MESH,
        )

    def start(step, carry):
        target = me + step

        @pl.when(target < count)
        def _():
            copy_between(me, target, target).start()

        return carry

    lax.fori_loop(1, count, start, 0)

    def finish(peer, carry):
        @pl.when(peer > me)
        def _():
            copy_between(me, peer, peer).wait_send()

        @pl.when(peer < me)
        def _():
            copy_between(peer, peer, peer).wait_recv()

        return carry

    lax.fori_loop(0, count, finish, 0)


def exchange(send):
    count = send.shape[0]
    return pl.pallas_call(
        functools.partial(exchange_kernel, count),
        out_shape=jax.ShapeDtypeStruct(send.shape, send.dtype),
        in_specs=[pl.BlockSpec(memory_space=pl.ANY)],
        out_specs=pl.BlockSpec(memory_space=pl.ANY),
        scratch_shapes=[
            pltpu.SemaphoreType.DMA((count,)),
            pltpu.SemaphoreType.DMA((count,)),
        ],
        compiler_params=pltpu.CompilerParams(collective_id=0, has_side_effects=True),
    )(send)


def attend_kernel(live_ref, q_ref, k_ref, v_ref, picked_ref, o_ref, out_buf, sems):
    head = pl.program_id(0)
    heads = pl.num_programs(0)
    rows = q_ref.shape[0]
    pipe_size = lax.axis_size("pipe")
    here = lax.axis_index("pipe")
    after = lax.rem(here + 1, pipe_size)
    before = lax.rem(here + pipe_size - 1, pipe_size)

    @pl.when(head == 0)
    def _():
        barrier = pltpu.get_barrier_semaphore()
        for peer in (before, after):
            pl.semaphore_signal(barrier, 1, device_id={"pipe": peer}, device_id_type=MESH)
        pl.semaphore_wait(barrier, 2)

    score_scale = HD ** (-0.5)
    dims = (((1,), (1,)), ((), ()))
    query = q_ref[...]

    def scores_against(key_rows):
        raw = lax.dot_general(query, key_rows, dims, preferred_element_type=jnp.float32)
        return raw * score_scale

    row_index = lax.broadcasted_iota(jnp.int32, (rows, rows), 0)
    col_index = lax.broadcasted_iota(jnp.int32, (rows, rows), 1)
    own = jnp.where(row_index >= col_index, scores_against(k_ref[...]), -jnp.inf)
    first_bias = jnp.where(live_ref[PICKS * head] > 0, 0.0, -jnp.inf)
    second_bias = jnp.where(live_ref[PICKS * head + 1] > 0, 0.0, -jnp.inf)
    first = scores_against(picked_ref[0, 0]) + first_bias
    second = scores_against(picked_ref[1, 0]) + second_bias
    row_top = jnp.maximum(
        jnp.maximum(jnp.max(own, axis=1), jnp.max(first, axis=1)), jnp.max(second, axis=1)
    )[:, None]
    own = jnp.exp(own - row_top)
    first = jnp.exp(first - row_top)
    second = jnp.exp(second - row_top)
    row_scale = 1.0 / (
        jnp.sum(own, axis=1) + jnp.sum(first, axis=1) + jnp.sum(second, axis=1)
    )[:, None]
    mixed = jnp.dot((own * row_scale).astype(jnp.bfloat16), v_ref[...],
                    preferred_element_type=jnp.float32)
    mixed += jnp.dot((first * row_scale).astype(jnp.bfloat16), picked_ref[0, 1],
                     preferred_element_type=jnp.float32)
    mixed += jnp.dot((second * row_scale).astype(jnp.bfloat16), picked_ref[1, 1],
                     preferred_element_type=jnp.float32)
    out_buf[head] = mixed.astype(out_buf.dtype)

    def relay(slot):
        return pltpu.make_async_remote_copy(
            src_ref=out_buf.at[slot],
            dst_ref=o_ref.at[:, pl.ds(pl.multiple_of(slot * HD, HD), HD)],
            send_sem=sems.at[0, slot],
            recv_sem=sems.at[1, slot],
            device_id={"pipe": after},
            device_id_type=MESH,
        )

    relay(head).start()

    @pl.when(head == heads - 1)
    def _():
        def finish(slot, carry):
            relay(slot).wait_send()
            relay(slot).wait_recv()
            return carry

        lax.fori_loop(0, heads, finish, 0)


def attend_and_pass(live, queries, keys, values, picked):
    rows = queries.shape[0]
    head_block = pl.BlockSpec((rows, HD), lambda h, live_ref: (0, h))
    grid_spec = pltpu.PrefetchScalarGridSpec(
        num_scalar_prefetch=1,
        grid=(HEADS,),
        in_specs=[
            head_block,
            head_block,
            head_block,
            pl.BlockSpec((PICKS, 2, rows, HD), lambda h, live_ref: (h, 0, 0, 0)),
        ],
        out_specs=pl.BlockSpec(memory_space=pl.ANY),
        scratch_shapes=[
            pltpu.VMEM((HEADS, rows, HD), queries.dtype),
            pltpu.SemaphoreType.DMA((2, HEADS)),
        ],
    )
    return pl.pallas_call(
        attend_kernel,
        grid_spec=grid_spec,
        out_shape=jax.ShapeDtypeStruct(queries.shape, queries.dtype),
        compiler_params=pltpu.CompilerParams(collective_id=0, has_side_effects=True),
    )(live, queries, keys, values, picked)


def gather_kernel(slot_ref, source_ref, out_ref, sems):
    count = out_ref.shape[0]

    def copy(i):
        return pltpu.make_async_copy(source_ref.at[slot_ref[i]], out_ref.at[i], sems.at[i])

    def start(i, carry):
        copy(i).start()
        return carry

    def finish(i, carry):
        copy(i).wait()
        return carry

    lax.fori_loop(0, count, start, 0)
    lax.fori_loop(0, count, finish, 0)


def gather_slots(slots, received):
    count = slots.shape[0]
    grid_spec = pltpu.PrefetchScalarGridSpec(
        num_scalar_prefetch=1,
        grid=(1,),
        in_specs=[pl.BlockSpec(memory_space=pl.ANY)],
        out_specs=pl.BlockSpec(memory_space=pl.ANY),
        scratch_shapes=[pltpu.SemaphoreType.DMA((count,))],
    )
    return pl.pallas_call(
        gather_kernel,
        grid_spec=grid_spec,
        out_shape=jax.ShapeDtypeStruct((count,) + received.shape[1:], received.dtype),
    )(slots, received)


def per_device(queries, keys, values, picks):
    rank_here = lax.axis_index("ctx")
    every_pick = picks[0]
    head_ids = lax.broadcasted_iota(jnp.int32, every_pick.shape, 1)
    asked = jnp.sum(jnp.where(every_pick == rank_here, head_ids, 0), axis=(1, 2))
    send = pack_requested(asked.astype(jnp.int32), keys[0], values[0])
    received = lax.all_to_all(send, "ctx", split_axis=0, concat_axis=0, tiled=True)
    chosen = lax.dynamic_index_in_dim(every_pick, rank_here, 0, keepdims=False).reshape(-1)
    live = (chosen >= 0).astype(jnp.int32)
    slots = jnp.maximum(chosen, 0).astype(jnp.int32)
    picked = gather_slots(slots, received)
    merged = attend_and_pass(live, queries[0], keys[0], values[0], picked)
    return merged[None]


def solution(mesh):
    placed = (
        P("pipe", "ctx", None),
        P("pipe", "ctx", None),
        P("pipe", "ctx", None),
        P("pipe", None, None, None),
    )
    return jax.shard_map(
        per_device, mesh=mesh, in_specs=placed, out_specs=P("pipe", "ctx", None), check_vma=False
    )
```

```python
import functools

import jax
import jax.numpy as jnp
from jax import lax
from jax.experimental import pallas as pl
from jax.experimental.pallas import tpu as pltpu
from jax.sharding import PartitionSpec as P

HEADS = 16
HD = 128
PICKS = 2
MESH = pl.DeviceIdType.MESH


def passed_along(value, axis, steps):
    count = lax.axis_size(axis)
    pairs = [(source, (source + steps) % count) for source in range(count)]
    return lax.ppermute(value, axis, pairs)


def pack_kernel(group, asked_ref, k_ref, v_ref, out_ref):
    base = pl.program_id(0) * group
    for i in range(group):
        column = pl.multiple_of(asked_ref[base + i] * HD, HD)
        out_ref[i, 0] = k_ref[:, pl.ds(column, HD)]
        out_ref[i, 1] = v_ref[:, pl.ds(column, HD)]


def pack_requested(asked, keys, values):
    count = asked.shape[0]
    rows, width = keys.shape
    group = 8
    whole = pl.BlockSpec((rows, width), lambda g, asked_ref: (0, 0))
    grid_spec = pltpu.PrefetchScalarGridSpec(
        num_scalar_prefetch=1,
        grid=(count // group,),
        in_specs=[whole, whole],
        out_specs=pl.BlockSpec((group, 2, rows, HD), lambda g, asked_ref: (g, 0, 0, 0)),
    )
    return pl.pallas_call(
        functools.partial(pack_kernel, group),
        grid_spec=grid_spec,
        out_shape=jax.ShapeDtypeStruct((count, 2, rows, HD), keys.dtype),
    )(asked, keys, values)


def exchange_kernel(count, send_ref, recv_ref, send_sems, recv_sems):
    me = lax.axis_index("ctx")
    barrier = pltpu.get_barrier_semaphore()

    def greet(step, carry):
        peer = lax.rem(me + step, count)
        pl.semaphore_signal(barrier, 1, device_id={"ctx": peer}, device_id_type=MESH)
        return carry

    lax.fori_loop(1, count, greet, 0)
    pl.semaphore_wait(barrier, count - 1)

    def copy_between(source, target, slot):
        return pltpu.make_async_remote_copy(
            src_ref=send_ref.at[slot],
            dst_ref=recv_ref.at[source],
            send_sem=send_sems.at[slot],
            recv_sem=recv_sems.at[source],
            device_id={"ctx": target},
            device_id_type=MESH,
        )

    def start(step, carry):
        target = me + step

        @pl.when(target < count)
        def _():
            copy_between(me, target, target).start()

        return carry

    lax.fori_loop(1, count, start, 0)

    def finish(peer, carry):
        @pl.when(peer > me)
        def _():
            copy_between(me, peer, peer).wait_send()

        @pl.when(peer < me)
        def _():
            copy_between(peer, peer, peer).wait_recv()

        return carry

    lax.fori_loop(0, count, finish, 0)


def exchange(send):
    count = send.shape[0]
    return pl.pallas_call(
        functools.partial(exchange_kernel, count),
        out_shape=jax.ShapeDtypeStruct(send.shape, send.dtype),
        in_specs=[pl.BlockSpec(memory_space=pl.ANY)],
        out_specs=pl.BlockSpec(memory_space=pl.ANY),
        scratch_shapes=[
            pltpu.SemaphoreType.DMA((count,)),
            pltpu.SemaphoreType.DMA((count,)),
        ],
        compiler_params=pltpu.CompilerParams(collective_id=0, has_side_effects=True),
    )(send)


def attend_kernel(slot_ref, live_ref, q_ref, k_ref, v_ref, received_ref, o_ref, out_buf, sems):
    head = pl.program_id(0)
    heads = pl.num_programs(0)
    rows = q_ref.shape[0]
    pipe_size = lax.axis_size("pipe")
    here = lax.axis_index("pipe")
    after = lax.rem(here + 1, pipe_size)
    before = lax.rem(here + pipe_size - 1, pipe_size)

    @pl.when(head == 0)
    def _():
        barrier = pltpu.get_barrier_semaphore()
        for peer in (before, after):
            pl.semaphore_signal(barrier, 1, device_id={"pipe": peer}, device_id_type=MESH)
        pl.semaphore_wait(barrier, 2)

    score_scale = HD ** (-0.5)
    dims = (((1,), (1,)), ((), ()))
    query = q_ref[...]

    def scores_against(key_rows):
        raw = lax.dot_general(query, key_rows, dims, preferred_element_type=jnp.float32)
        return raw * score_scale

    row_index = lax.broadcasted_iota(jnp.int32, (rows, rows), 0)
    col_index = lax.broadcasted_iota(jnp.int32, (rows, rows), 1)
    own = jnp.where(row_index >= col_index, scores_against(k_ref[...]), -jnp.inf)
    first_bias = jnp.where(live_ref[PICKS * head] > 0, 0.0, -jnp.inf)
    second_bias = jnp.where(live_ref[PICKS * head + 1] > 0, 0.0, -jnp.inf)
    first_block = received_ref[slot_ref[PICKS * head]]
    second_block = received_ref[slot_ref[PICKS * head + 1]]
    first = scores_against(first_block[0]) + first_bias
    second = scores_against(second_block[0]) + second_bias
    row_top = jnp.maximum(
        jnp.maximum(jnp.max(own, axis=1), jnp.max(first, axis=1)), jnp.max(second, axis=1)
    )[:, None]
    own = jnp.exp(own - row_top)
    first = jnp.exp(first - row_top)
    second = jnp.exp(second - row_top)
    row_scale = 1.0 / (
        jnp.sum(own, axis=1) + jnp.sum(first, axis=1) + jnp.sum(second, axis=1)
    )[:, None]
    mixed = jnp.dot((own * row_scale).astype(jnp.bfloat16), v_ref[...],
                    preferred_element_type=jnp.float32)
    mixed += jnp.dot((first * row_scale).astype(jnp.bfloat16), first_block[1],
                     preferred_element_type=jnp.float32)
    mixed += jnp.dot((second * row_scale).astype(jnp.bfloat16), second_block[1],
                     preferred_element_type=jnp.float32)
    out_buf[head] = mixed.astype(out_buf.dtype)

    def relay(slot):
        return pltpu.make_async_remote_copy(
            src_ref=out_buf.at[slot],
            dst_ref=o_ref.at[:, pl.ds(pl.multiple_of(slot * HD, HD), HD)],
            send_sem=sems.at[0, slot],
            recv_sem=sems.at[1, slot],
            device_id={"pipe": after},
            device_id_type=MESH,
        )

    relay(head).start()

    @pl.when(head == heads - 1)
    def _():
        def finish(slot, carry):
            relay(slot).wait_send()
            relay(slot).wait_recv()
            return carry

        lax.fori_loop(0, heads, finish, 0)


def attend_and_pass(slots, live, queries, keys, values, received):
    rows = queries.shape[0]
    head_block = pl.BlockSpec((rows, HD), lambda h, slot_ref, live_ref: (0, h))
    grid_spec = pltpu.PrefetchScalarGridSpec(
        num_scalar_prefetch=2,
        grid=(HEADS,),
        in_specs=[
            head_block,
            head_block,
            head_block,
            pl.BlockSpec(memory_space=pltpu.VMEM),
        ],
        out_specs=pl.BlockSpec(memory_space=pl.ANY),
        scratch_shapes=[
            pltpu.VMEM((HEADS, rows, HD), queries.dtype),
            pltpu.SemaphoreType.DMA((2, HEADS)),
        ],
    )
    return pl.pallas_call(
        attend_kernel,
        grid_spec=grid_spec,
        out_shape=jax.ShapeDtypeStruct(queries.shape, queries.dtype),
        compiler_params=pltpu.CompilerParams(
            collective_id=0, has_side_effects=True, vmem_limit_bytes=48 * 1024 * 1024
        ),
    )(slots, live, queries, keys, values, received)


def per_device(queries, keys, values, picks):
    rank_here = lax.axis_index("ctx")
    every_pick = picks[0]
    head_ids = lax.broadcasted_iota(jnp.int32, every_pick.shape, 1)
    asked = jnp.sum(jnp.where(every_pick == rank_here, head_ids, 0), axis=(1, 2))
    send = pack_requested(asked.astype(jnp.int32), keys[0], values[0])
    received = lax.all_to_all(send, "ctx", split_axis=0, concat_axis=0, tiled=True)
    chosen = lax.dynamic_index_in_dim(every_pick, rank_here, 0, keepdims=False).reshape(-1)
    live = (chosen >= 0).astype(jnp.int32)
    slots = jnp.maximum(chosen, 0).astype(jnp.int32)
    merged = attend_and_pass(slots, live, queries[0], keys[0], values[0], received)
    return merged[None]


def solution(mesh):
    placed = (
        P("pipe", "ctx", None),
        P("pipe", "ctx", None),
        P("pipe", "ctx", None),
        P("pipe", None, None, None),
    )
    return jax.shard_map(
        per_device, mesh=mesh, in_specs=placed, out_specs=P("pipe", "ctx", None), check_vma=False
    )
```

```python
import functools

import jax
import jax.numpy as jnp
from jax import lax
from jax.experimental import pallas as pl
from jax.experimental.pallas import tpu as pltpu
from jax.sharding import PartitionSpec as P

HEADS = 16
HD = 128
PICKS = 2
MESH = pl.DeviceIdType.MESH


def passed_along(value, axis, steps):
    count = lax.axis_size(axis)
    pairs = [(source, (source + steps) % count) for source in range(count)]
    return lax.ppermute(value, axis, pairs)


def pack_kernel(group, asked_ref, k_ref, v_ref, out_ref):
    base = pl.program_id(0) * group
    for i in range(group):
        column = pl.multiple_of(asked_ref[base + i] * HD, HD)
        out_ref[i, 0] = k_ref[:, pl.ds(column, HD)]
        out_ref[i, 1] = v_ref[:, pl.ds(column, HD)]


def pack_requested(asked, keys, values):
    count = asked.shape[0]
    rows, width = keys.shape
    group = 8
    whole = pl.BlockSpec((rows, width), lambda g, asked_ref: (0, 0))
    grid_spec = pltpu.PrefetchScalarGridSpec(
        num_scalar_prefetch=1,
        grid=(count // group,),
        in_specs=[whole, whole],
        out_specs=pl.BlockSpec((group, 2, rows, HD), lambda g, asked_ref: (g, 0, 0, 0)),
    )
    return pl.pallas_call(
        functools.partial(pack_kernel, group),
        grid_spec=grid_spec,
        out_shape=jax.ShapeDtypeStruct((count, 2, rows, HD), keys.dtype),
    )(asked, keys, values)


def exchange_kernel(count, send_ref, recv_ref, send_sems, recv_sems):
    me = lax.axis_index("ctx")
    barrier = pltpu.get_barrier_semaphore()

    def greet(step, carry):
        peer = lax.rem(me + step, count)
        pl.semaphore_signal(barrier, 1, device_id={"ctx": peer}, device_id_type=MESH)
        return carry

    lax.fori_loop(1, count, greet, 0)
    pl.semaphore_wait(barrier, count - 1)

    def copy_between(source, target, slot):
        return pltpu.make_async_remote_copy(
            src_ref=send_ref.at[slot],
            dst_ref=recv_ref.at[source],
            send_sem=send_sems.at[slot],
            recv_sem=recv_sems.at[source],
            device_id={"ctx": target},
            device_id_type=MESH,
        )

    def start(step, carry):
        target = me + step

        @pl.when(target < count)
        def _():
            copy_between(me, target, target).start()

        return carry

    lax.fori_loop(1, count, start, 0)

    def finish(peer, carry):
        @pl.when(peer > me)
        def _():
            copy_between(me, peer, peer).wait_send()

        @pl.when(peer < me)
        def _():
            copy_between(peer, peer, peer).wait_recv()

        return carry

    lax.fori_loop(0, count, finish, 0)


def exchange(send):
    count = send.shape[0]
    return pl.pallas_call(
        functools.partial(exchange_kernel, count),
        out_shape=jax.ShapeDtypeStruct(send.shape, send.dtype),
        in_specs=[pl.BlockSpec(memory_space=pl.ANY)],
        out_specs=pl.BlockSpec(memory_space=pl.ANY),
        scratch_shapes=[
            pltpu.SemaphoreType.DMA((count,)),
            pltpu.SemaphoreType.DMA((count,)),
        ],
        compiler_params=pltpu.CompilerParams(collective_id=0, has_side_effects=True),
    )(send)


def attend_kernel(slot_ref, live_ref, q_ref, k_ref, v_ref, received_ref, o_ref, out_buf, sems):
    head = pl.program_id(0)
    heads = pl.num_programs(0)
    rows = q_ref.shape[0]
    pipe_size = lax.axis_size("pipe")
    here = lax.axis_index("pipe")
    after = lax.rem(here + 1, pipe_size)
    before = lax.rem(here + pipe_size - 1, pipe_size)

    @pl.when(head == 0)
    def _():
        barrier = pltpu.get_barrier_semaphore()
        for peer in (before, after):
            pl.semaphore_signal(barrier, 1, device_id={"pipe": peer}, device_id_type=MESH)
        pl.semaphore_wait(barrier, 2)

    score_scale = HD ** (-0.5)
    dims = (((1,), (1,)), ((), ()))
    first_bias = jnp.where(live_ref[PICKS * head] > 0, 0.0, -jnp.inf)
    second_bias = jnp.where(live_ref[PICKS * head + 1] > 0, 0.0, -jnp.inf)
    first_block = received_ref[slot_ref[PICKS * head]]
    second_block = received_ref[slot_ref[PICKS * head + 1]]
    half = rows // 2
    for part in range(2):
        low = part * half
        width = low + half
        query = q_ref[low:low + half, :]

        def scores_against(key_rows, query=query):
            raw = lax.dot_general(query, key_rows, dims, preferred_element_type=jnp.float32)
            return raw * score_scale

        row_index = lax.broadcasted_iota(jnp.int32, (half, width), 0) + low
        col_index = lax.broadcasted_iota(jnp.int32, (half, width), 1)
        own = jnp.where(row_index >= col_index, scores_against(k_ref[:width, :]), -jnp.inf)
        first = scores_against(first_block[0]) + first_bias
        second = scores_against(second_block[0]) + second_bias
        row_top = jnp.maximum(
            jnp.maximum(jnp.max(own, axis=1), jnp.max(first, axis=1)), jnp.max(second, axis=1)
        )[:, None]
        own = jnp.exp(own - row_top)
        first = jnp.exp(first - row_top)
        second = jnp.exp(second - row_top)
        row_scale = 1.0 / (
            jnp.sum(own, axis=1) + jnp.sum(first, axis=1) + jnp.sum(second, axis=1)
        )[:, None]
        mixed = jnp.dot((own * row_scale).astype(jnp.bfloat16), v_ref[:width, :],
                        preferred_element_type=jnp.float32)
        mixed += jnp.dot((first * row_scale).astype(jnp.bfloat16), first_block[1],
                         preferred_element_type=jnp.float32)
        mixed += jnp.dot((second * row_scale).astype(jnp.bfloat16), second_block[1],
                         preferred_element_type=jnp.float32)
        out_buf[head, low:low + half, :] = mixed.astype(out_buf.dtype)

    def relay(slot):
        return pltpu.make_async_remote_copy(
            src_ref=out_buf.at[slot],
            dst_ref=o_ref.at[:, pl.ds(pl.multiple_of(slot * HD, HD), HD)],
            send_sem=sems.at[0, slot],
            recv_sem=sems.at[1, slot],
            device_id={"pipe": after},
            device_id_type=MESH,
        )

    relay(head).start()

    @pl.when(head == heads - 1)
    def _():
        def finish(slot, carry):
            relay(slot).wait_send()
            relay(slot).wait_recv()
            return carry

        lax.fori_loop(0, heads, finish, 0)


def attend_and_pass(slots, live, queries, keys, values, received):
    rows = queries.shape[0]
    head_block = pl.BlockSpec((rows, HD), lambda h, slot_ref, live_ref: (0, h))
    grid_spec = pltpu.PrefetchScalarGridSpec(
        num_scalar_prefetch=2,
        grid=(HEADS,),
        in_specs=[
            head_block,
            head_block,
            head_block,
            pl.BlockSpec(memory_space=pltpu.VMEM),
        ],
        out_specs=pl.BlockSpec(memory_space=pl.ANY),
        scratch_shapes=[
            pltpu.VMEM((HEADS, rows, HD), queries.dtype),
            pltpu.SemaphoreType.DMA((2, HEADS)),
        ],
    )
    return pl.pallas_call(
        attend_kernel,
        grid_spec=grid_spec,
        out_shape=jax.ShapeDtypeStruct(queries.shape, queries.dtype),
        compiler_params=pltpu.CompilerParams(
            collective_id=0, has_side_effects=True, vmem_limit_bytes=48 * 1024 * 1024
        ),
    )(slots, live, queries, keys, values, received)


def per_device(queries, keys, values, picks):
    rank_here = lax.axis_index("ctx")
    every_pick = picks[0]
    head_ids = lax.broadcasted_iota(jnp.int32, every_pick.shape, 1)
    asked = jnp.sum(jnp.where(every_pick == rank_here, head_ids, 0), axis=(1, 2))
    send = pack_requested(asked.astype(jnp.int32), keys[0], values[0])
    received = lax.all_to_all(send, "ctx", split_axis=0, concat_axis=0, tiled=True)
    chosen = lax.dynamic_index_in_dim(every_pick, rank_here, 0, keepdims=False).reshape(-1)
    live = (chosen >= 0).astype(jnp.int32)
    slots = jnp.maximum(chosen, 0).astype(jnp.int32)
    merged = attend_and_pass(slots, live, queries[0], keys[0], values[0], received)
    return merged[None]


def solution(mesh):
    placed = (
        P("pipe", "ctx", None),
        P("pipe", "ctx", None),
        P("pipe", "ctx", None),
        P("pipe", None, None, None),
    )
    return jax.shard_map(
        per_device, mesh=mesh, in_specs=placed, out_specs=P("pipe", "ctx", None), check_vma=False
    )
```

```python
import functools

import jax
import jax.numpy as jnp
from jax import lax
from jax.experimental import pallas as pl
from jax.experimental.pallas import tpu as pltpu
from jax.sharding import PartitionSpec as P

HEADS = 16
HD = 128
PICKS = 2
MESH = pl.DeviceIdType.MESH


def passed_along(value, axis, steps):
    count = lax.axis_size(axis)
    pairs = [(source, (source + steps) % count) for source in range(count)]
    return lax.ppermute(value, axis, pairs)


def pack_kernel(group, asked_ref, source_ref, out_ref):
    base = pl.program_id(0) * group
    for i in range(group):
        column = pl.multiple_of(asked_ref[base + i] * HD, HD)
        out_ref[i] = source_ref[:, pl.ds(column, HD)]


def pack_requested(asked, source):
    count = asked.shape[0]
    rows, width = source.shape
    group = 8
    grid_spec = pltpu.PrefetchScalarGridSpec(
        num_scalar_prefetch=1,
        grid=(count // group,),
        in_specs=[pl.BlockSpec((rows, width), lambda g, asked_ref: (0, 0))],
        out_specs=pl.BlockSpec((group, rows, HD), lambda g, asked_ref: (g, 0, 0)),
    )
    return pl.pallas_call(
        functools.partial(pack_kernel, group),
        grid_spec=grid_spec,
        out_shape=jax.ShapeDtypeStruct((count, rows, HD), source.dtype),
    )(asked, source)


def exchange_kernel(count, send_ref, recv_ref, send_sems, recv_sems):
    me = lax.axis_index("ctx")
    barrier = pltpu.get_barrier_semaphore()

    def greet(step, carry):
        peer = lax.rem(me + step, count)
        pl.semaphore_signal(barrier, 1, device_id={"ctx": peer}, device_id_type=MESH)
        return carry

    lax.fori_loop(1, count, greet, 0)
    pl.semaphore_wait(barrier, count - 1)

    def copy_between(source, target, slot):
        return pltpu.make_async_remote_copy(
            src_ref=send_ref.at[slot],
            dst_ref=recv_ref.at[source],
            send_sem=send_sems.at[slot],
            recv_sem=recv_sems.at[source],
            device_id={"ctx": target},
            device_id_type=MESH,
        )

    def start(step, carry):
        target = me + step

        @pl.when(target < count)
        def _():
            copy_between(me, target, target).start()

        return carry

    lax.fori_loop(1, count, start, 0)

    def finish(peer, carry):
        @pl.when(peer > me)
        def _():
            copy_between(me, peer, peer).wait_send()

        @pl.when(peer < me)
        def _():
            copy_between(peer, peer, peer).wait_recv()

        return carry

    lax.fori_loop(0, count, finish, 0)


def exchange(send):
    count = send.shape[0]
    return pl.pallas_call(
        functools.partial(exchange_kernel, count),
        out_shape=jax.ShapeDtypeStruct(send.shape, send.dtype),
        in_specs=[pl.BlockSpec(memory_space=pl.ANY)],
        out_specs=pl.BlockSpec(memory_space=pl.ANY),
        scratch_shapes=[
            pltpu.SemaphoreType.DMA((count,)),
            pltpu.SemaphoreType.DMA((count,)),
        ],
        compiler_params=pltpu.CompilerParams(collective_id=0, has_side_effects=True),
    )(send)


def attend_kernel(slot_ref, live_ref, q_ref, k_ref, v_ref, got_keys_ref, got_values_ref, o_ref,
                  out_buf, sems):
    head = pl.program_id(0)
    heads = pl.num_programs(0)
    rows = q_ref.shape[0]
    pipe_size = lax.axis_size("pipe")
    here = lax.axis_index("pipe")
    after = lax.rem(here + 1, pipe_size)
    before = lax.rem(here + pipe_size - 1, pipe_size)

    @pl.when(head == 0)
    def _():
        barrier = pltpu.get_barrier_semaphore()
        for peer in (before, after):
            pl.semaphore_signal(barrier, 1, device_id={"pipe": peer}, device_id_type=MESH)
        pl.semaphore_wait(barrier, 2)

    score_scale = HD ** (-0.5)
    dims = (((1,), (1,)), ((), ()))
    first_bias = jnp.where(live_ref[PICKS * head] > 0, 0.0, -jnp.inf)
    second_bias = jnp.where(live_ref[PICKS * head + 1] > 0, 0.0, -jnp.inf)
    first_slot = slot_ref[PICKS * head]
    second_slot = slot_ref[PICKS * head + 1]
    first_block = (got_keys_ref[first_slot], got_values_ref[first_slot])
    second_block = (got_keys_ref[second_slot], got_values_ref[second_slot])
    half = rows // 2
    for part in range(2):
        low = part * half
        width = low + half
        query = q_ref[low:low + half, :]

        def scores_against(key_rows, query=query):
            raw = lax.dot_general(query, key_rows, dims, preferred_element_type=jnp.float32)
            return raw * score_scale

        row_index = lax.broadcasted_iota(jnp.int32, (half, width), 0) + low
        col_index = lax.broadcasted_iota(jnp.int32, (half, width), 1)
        own = jnp.where(row_index >= col_index, scores_against(k_ref[:width, :]), -jnp.inf)
        first = scores_against(first_block[0]) + first_bias
        second = scores_against(second_block[0]) + second_bias
        row_top = jnp.maximum(
            jnp.maximum(jnp.max(own, axis=1), jnp.max(first, axis=1)), jnp.max(second, axis=1)
        )[:, None]
        own = jnp.exp(own - row_top)
        first = jnp.exp(first - row_top)
        second = jnp.exp(second - row_top)
        row_scale = 1.0 / (
            jnp.sum(own, axis=1) + jnp.sum(first, axis=1) + jnp.sum(second, axis=1)
        )[:, None]
        mixed = jnp.dot((own * row_scale).astype(jnp.bfloat16), v_ref[:width, :],
                        preferred_element_type=jnp.float32)
        mixed += jnp.dot((first * row_scale).astype(jnp.bfloat16), first_block[1],
                         preferred_element_type=jnp.float32)
        mixed += jnp.dot((second * row_scale).astype(jnp.bfloat16), second_block[1],
                         preferred_element_type=jnp.float32)
        out_buf[head, low:low + half, :] = mixed.astype(out_buf.dtype)

    def relay(slot):
        return pltpu.make_async_remote_copy(
            src_ref=out_buf.at[slot],
            dst_ref=o_ref.at[:, pl.ds(pl.multiple_of(slot * HD, HD), HD)],
            send_sem=sems.at[0, slot],
            recv_sem=sems.at[1, slot],
            device_id={"pipe": after},
            device_id_type=MESH,
        )

    relay(head).start()

    @pl.when(head == heads - 1)
    def _():
        def finish(slot, carry):
            relay(slot).wait_send()
            relay(slot).wait_recv()
            return carry

        lax.fori_loop(0, heads, finish, 0)


def attend_and_pass(slots, live, queries, keys, values, got_keys, got_values):
    rows = queries.shape[0]
    head_block = pl.BlockSpec((rows, HD), lambda h, slot_ref, live_ref: (0, h))
    grid_spec = pltpu.PrefetchScalarGridSpec(
        num_scalar_prefetch=2,
        grid=(HEADS,),
        in_specs=[
            head_block,
            head_block,
            head_block,
            pl.BlockSpec(memory_space=pltpu.VMEM),
            pl.BlockSpec(memory_space=pltpu.VMEM),
        ],
        out_specs=pl.BlockSpec(memory_space=pl.ANY),
        scratch_shapes=[
            pltpu.VMEM((HEADS, rows, HD), queries.dtype),
            pltpu.SemaphoreType.DMA((2, HEADS)),
        ],
    )
    return pl.pallas_call(
        attend_kernel,
        grid_spec=grid_spec,
        out_shape=jax.ShapeDtypeStruct(queries.shape, queries.dtype),
        compiler_params=pltpu.CompilerParams(
            collective_id=0, has_side_effects=True, vmem_limit_bytes=48 * 1024 * 1024
        ),
    )(slots, live, queries, keys, values, got_keys, got_values)


def per_device(queries, keys, values, picks):
    rank_here = lax.axis_index("ctx")
    every_pick = picks[0]
    head_ids = lax.broadcasted_iota(jnp.int32, every_pick.shape, 1)
    asked = jnp.sum(jnp.where(every_pick == rank_here, head_ids, 0), axis=(1, 2))
    asked = asked.astype(jnp.int32)
    got_keys = lax.all_to_all(pack_requested(asked, keys[0]), "ctx", split_axis=0, concat_axis=0,
                              tiled=True)
    got_values = lax.all_to_all(pack_requested(asked, values[0]), "ctx", split_axis=0,
                                concat_axis=0, tiled=True)
    chosen = lax.dynamic_index_in_dim(every_pick, rank_here, 0, keepdims=False).reshape(-1)
    live = (chosen >= 0).astype(jnp.int32)
    slots = jnp.maximum(chosen, 0).astype(jnp.int32)
    merged = attend_and_pass(slots, live, queries[0], keys[0], values[0], got_keys, got_values)
    return merged[None]


def solution(mesh):
    placed = (
        P("pipe", "ctx", None),
        P("pipe", "ctx", None),
        P("pipe", "ctx", None),
        P("pipe", None, None, None),
    )
    return jax.shard_map(
        per_device, mesh=mesh, in_specs=placed, out_specs=P("pipe", "ctx", None), check_vma=False
    )
```

```python
import functools

import jax
import jax.numpy as jnp
from jax import lax
from jax.experimental import pallas as pl
from jax.experimental.pallas import tpu as pltpu
from jax.sharding import PartitionSpec as P

HEADS = 16
HD = 128
PICKS = 2
MESH = pl.DeviceIdType.MESH


def passed_along(value, axis, steps):
    count = lax.axis_size(axis)
    pairs = [(source, (source + steps) % count) for source in range(count)]
    return lax.ppermute(value, axis, pairs)


def pack_kernel(group, asked_ref, k_ref, v_ref, out_ref):
    base = pl.program_id(0) * group
    for i in range(group):
        column = pl.multiple_of(asked_ref[base + i] * HD, HD)
        out_ref[i, 0] = k_ref[:, pl.ds(column, HD)]
        out_ref[i, 1] = v_ref[:, pl.ds(column, HD)]


def pack_requested(asked, keys, values):
    count = asked.shape[0]
    rows, width = keys.shape
    group = 16
    whole = pl.BlockSpec((rows, width), lambda g, asked_ref: (0, 0))
    grid_spec = pltpu.PrefetchScalarGridSpec(
        num_scalar_prefetch=1,
        grid=(count // group,),
        in_specs=[whole, whole],
        out_specs=pl.BlockSpec((group, 2, rows, HD), lambda g, asked_ref: (g, 0, 0, 0)),
    )
    return pl.pallas_call(
        functools.partial(pack_kernel, group),
        grid_spec=grid_spec,
        out_shape=jax.ShapeDtypeStruct((count, 2, rows, HD), keys.dtype),
    )(asked, keys, values)


def exchange_kernel(count, send_ref, recv_ref, send_sems, recv_sems):
    me = lax.axis_index("ctx")
    barrier = pltpu.get_barrier_semaphore()

    def greet(step, carry):
        peer = lax.rem(me + step, count)
        pl.semaphore_signal(barrier, 1, device_id={"ctx": peer}, device_id_type=MESH)
        return carry

    lax.fori_loop(1, count, greet, 0)
    pl.semaphore_wait(barrier, count - 1)

    def copy_between(source, target, slot):
        return pltpu.make_async_remote_copy(
            src_ref=send_ref.at[slot],
            dst_ref=recv_ref.at[source],
            send_sem=send_sems.at[slot],
            recv_sem=recv_sems.at[source],
            device_id={"ctx": target},
            device_id_type=MESH,
        )

    def start(step, carry):
        target = me + step

        @pl.when(target < count)
        def _():
            copy_between(me, target, target).start()

        return carry

    lax.fori_loop(1, count, start, 0)

    def finish(peer, carry):
        @pl.when(peer > me)
        def _():
            copy_between(me, peer, peer).wait_send()

        @pl.when(peer < me)
        def _():
            copy_between(peer, peer, peer).wait_recv()

        return carry

    lax.fori_loop(0, count, finish, 0)


def exchange(send):
    count = send.shape[0]
    return pl.pallas_call(
        functools.partial(exchange_kernel, count),
        out_shape=jax.ShapeDtypeStruct(send.shape, send.dtype),
        in_specs=[pl.BlockSpec(memory_space=pl.ANY)],
        out_specs=pl.BlockSpec(memory_space=pl.ANY),
        scratch_shapes=[
            pltpu.SemaphoreType.DMA((count,)),
            pltpu.SemaphoreType.DMA((count,)),
        ],
        compiler_params=pltpu.CompilerParams(collective_id=0, has_side_effects=True),
    )(send)


def attend_kernel(slot_ref, live_ref, q_ref, k_ref, v_ref, received_ref, o_ref, out_buf, sems):
    head = pl.program_id(0)
    heads = pl.num_programs(0)
    rows = q_ref.shape[0]
    pipe_size = lax.axis_size("pipe")
    here = lax.axis_index("pipe")
    after = lax.rem(here + 1, pipe_size)
    before = lax.rem(here + pipe_size - 1, pipe_size)

    @pl.when(head == 0)
    def _():
        barrier = pltpu.get_barrier_semaphore()
        for peer in (before, after):
            pl.semaphore_signal(barrier, 1, device_id={"pipe": peer}, device_id_type=MESH)
        pl.semaphore_wait(barrier, 2)

    score_scale = HD ** (-0.5)
    dims = (((1,), (1,)), ((), ()))
    first_bias = jnp.where(live_ref[PICKS * head] > 0, 0.0, -jnp.inf)
    second_bias = jnp.where(live_ref[PICKS * head + 1] > 0, 0.0, -jnp.inf)
    first_block = received_ref[slot_ref[PICKS * head]]
    second_block = received_ref[slot_ref[PICKS * head + 1]]
    half = rows // 2
    for part in range(2):
        low = part * half
        width = low + half
        query = q_ref[low:low + half, :]

        def scores_against(key_rows, query=query):
            raw = lax.dot_general(query, key_rows, dims, preferred_element_type=jnp.float32)
            return raw * score_scale

        row_index = lax.broadcasted_iota(jnp.int32, (half, width), 0) + low
        col_index = lax.broadcasted_iota(jnp.int32, (half, width), 1)
        own = jnp.where(row_index >= col_index, scores_against(k_ref[:width, :]), -jnp.inf)
        first = scores_against(first_block[0]) + first_bias
        second = scores_against(second_block[0]) + second_bias
        row_top = jnp.maximum(
            jnp.maximum(jnp.max(own, axis=1), jnp.max(first, axis=1)), jnp.max(second, axis=1)
        )[:, None]
        own = jnp.exp(own - row_top)
        first = jnp.exp(first - row_top)
        second = jnp.exp(second - row_top)
        row_scale = 1.0 / (
            jnp.sum(own, axis=1) + jnp.sum(first, axis=1) + jnp.sum(second, axis=1)
        )[:, None]
        mixed = jnp.dot((own * row_scale).astype(jnp.bfloat16), v_ref[:width, :],
                        preferred_element_type=jnp.float32)
        mixed += jnp.dot((first * row_scale).astype(jnp.bfloat16), first_block[1],
                         preferred_element_type=jnp.float32)
        mixed += jnp.dot((second * row_scale).astype(jnp.bfloat16), second_block[1],
                         preferred_element_type=jnp.float32)
        out_buf[head, low:low + half, :] = mixed.astype(out_buf.dtype)

    def relay(slot):
        return pltpu.make_async_remote_copy(
            src_ref=out_buf.at[slot],
            dst_ref=o_ref.at[:, pl.ds(pl.multiple_of(slot * HD, HD), HD)],
            send_sem=sems.at[0, slot],
            recv_sem=sems.at[1, slot],
            device_id={"pipe": after},
            device_id_type=MESH,
        )

    relay(head).start()

    @pl.when(head == heads - 1)
    def _():
        def finish(slot, carry):
            relay(slot).wait_send()
            relay(slot).wait_recv()
            return carry

        lax.fori_loop(0, heads, finish, 0)


def attend_and_pass(slots, live, queries, keys, values, received):
    rows = queries.shape[0]
    head_block = pl.BlockSpec((rows, HD), lambda h, slot_ref, live_ref: (0, h))
    grid_spec = pltpu.PrefetchScalarGridSpec(
        num_scalar_prefetch=2,
        grid=(HEADS,),
        in_specs=[
            head_block,
            head_block,
            head_block,
            pl.BlockSpec(memory_space=pltpu.VMEM),
        ],
        out_specs=pl.BlockSpec(memory_space=pl.ANY),
        scratch_shapes=[
            pltpu.VMEM((HEADS, rows, HD), queries.dtype),
            pltpu.SemaphoreType.DMA((2, HEADS)),
        ],
    )
    return pl.pallas_call(
        attend_kernel,
        grid_spec=grid_spec,
        out_shape=jax.ShapeDtypeStruct(queries.shape, queries.dtype),
        compiler_params=pltpu.CompilerParams(
            collective_id=0, has_side_effects=True, vmem_limit_bytes=48 * 1024 * 1024
        ),
    )(slots, live, queries, keys, values, received)


def per_device(queries, keys, values, picks):
    rank_here = lax.axis_index("ctx")
    every_pick = picks[0]
    head_ids = lax.broadcasted_iota(jnp.int32, every_pick.shape, 1)
    asked = jnp.sum(jnp.where(every_pick == rank_here, head_ids, 0), axis=(1, 2))
    send = pack_requested(asked.astype(jnp.int32), keys[0], values[0])
    received = lax.all_to_all(send, "ctx", split_axis=0, concat_axis=0, tiled=True)
    chosen = lax.dynamic_index_in_dim(every_pick, rank_here, 0, keepdims=False).reshape(-1)
    live = (chosen >= 0).astype(jnp.int32)
    slots = jnp.maximum(chosen, 0).astype(jnp.int32)
    merged = attend_and_pass(slots, live, queries[0], keys[0], values[0], received)
    return merged[None]


def solution(mesh):
    placed = (
        P("pipe", "ctx", None),
        P("pipe", "ctx", None),
        P("pipe", "ctx", None),
        P("pipe", None, None, None),
    )
    return jax.shard_map(
        per_device, mesh=mesh, in_specs=placed, out_specs=P("pipe", "ctx", None), check_vma=False
    )
```

```python
import functools

import jax
import jax.numpy as jnp
from jax import lax
from jax.experimental import pallas as pl
from jax.experimental.pallas import tpu as pltpu
from jax.sharding import PartitionSpec as P

HEADS = 16
HD = 128
PICKS = 2
MESH = pl.DeviceIdType.MESH


def passed_along(value, axis, steps):
    count = lax.axis_size(axis)
    pairs = [(source, (source + steps) % count) for source in range(count)]
    return lax.ppermute(value, axis, pairs)


def pack_kernel(group, asked_ref, k_ref, v_ref, out_ref):
    base = pl.program_id(0) * group
    for i in range(group):
        column = pl.multiple_of(asked_ref[base + i] * HD, HD)
        out_ref[i, 0] = k_ref[:, pl.ds(column, HD)]
        out_ref[i, 1] = v_ref[:, pl.ds(column, HD)]


def pack_requested(asked, keys, values):
    count = asked.shape[0]
    rows, width = keys.shape
    group = 8
    whole = pl.BlockSpec((rows, width), lambda g, asked_ref: (0, 0))
    grid_spec = pltpu.PrefetchScalarGridSpec(
        num_scalar_prefetch=1,
        grid=(count // group,),
        in_specs=[whole, whole],
        out_specs=pl.BlockSpec((group, 2, rows, HD), lambda g, asked_ref: (g, 0, 0, 0)),
    )
    return pl.pallas_call(
        functools.partial(pack_kernel, group),
        grid_spec=grid_spec,
        out_shape=jax.ShapeDtypeStruct((count, 2, rows, HD), keys.dtype),
    )(asked, keys, values)


def exchange_kernel(count, send_ref, recv_ref, send_sems, recv_sems):
    me = lax.axis_index("ctx")
    barrier = pltpu.get_barrier_semaphore()

    def greet(step, carry):
        peer = lax.rem(me + step, count)
        pl.semaphore_signal(barrier, 1, device_id={"ctx": peer}, device_id_type=MESH)
        return carry

    lax.fori_loop(1, count, greet, 0)
    pl.semaphore_wait(barrier, count - 1)

    def copy_between(source, target, slot):
        return pltpu.make_async_remote_copy(
            src_ref=send_ref.at[slot],
            dst_ref=recv_ref.at[source],
            send_sem=send_sems.at[slot],
            recv_sem=recv_sems.at[source],
            device_id={"ctx": target},
            device_id_type=MESH,
        )

    def start(step, carry):
        target = me + step

        @pl.when(target < count)
        def _():
            copy_between(me, target, target).start()

        return carry

    lax.fori_loop(1, count, start, 0)

    def finish(peer, carry):
        @pl.when(peer > me)
        def _():
            copy_between(me, peer, peer).wait_send()

        @pl.when(peer < me)
        def _():
            copy_between(peer, peer, peer).wait_recv()

        return carry

    lax.fori_loop(0, count, finish, 0)


def exchange(send):
    count = send.shape[0]
    return pl.pallas_call(
        functools.partial(exchange_kernel, count),
        out_shape=jax.ShapeDtypeStruct(send.shape, send.dtype),
        in_specs=[pl.BlockSpec(memory_space=pl.ANY)],
        out_specs=pl.BlockSpec(memory_space=pl.ANY),
        scratch_shapes=[
            pltpu.SemaphoreType.DMA((count,)),
            pltpu.SemaphoreType.DMA((count,)),
        ],
        compiler_params=pltpu.CompilerParams(collective_id=0, has_side_effects=True),
    )(send)


def attend_kernel(slot_ref, live_ref, q_ref, k_ref, v_ref, received_ref, o_ref, out_buf, sems):
    step = pl.program_id(0)
    steps = pl.num_programs(0)
    heads = out_buf.shape[0]
    rows = q_ref.shape[0]
    pipe_size = lax.axis_size("pipe")
    here = lax.axis_index("pipe")
    after = lax.rem(here + 1, pipe_size)
    before = lax.rem(here + pipe_size - 1, pipe_size)

    @pl.when(step == 0)
    def _():
        barrier = pltpu.get_barrier_semaphore()
        for peer in (before, after):
            pl.semaphore_signal(barrier, 1, device_id={"pipe": peer}, device_id_type=MESH)
        pl.semaphore_wait(barrier, 2)

    def relay(slot):
        return pltpu.make_async_remote_copy(
            src_ref=out_buf.at[slot],
            dst_ref=o_ref.at[:, pl.ds(pl.multiple_of(slot * HD, HD), HD)],
            send_sem=sems.at[0, slot],
            recv_sem=sems.at[1, slot],
            device_id={"pipe": after},
            device_id_type=MESH,
        )

    score_scale = HD ** (-0.5)
    dims = (((1,), (1,)), ((), ()))
    per_step = q_ref.shape[1] // HD
    for inner in range(per_step):
        slot = step * per_step + inner
        lanes = slice(inner * HD, (inner + 1) * HD)
        first_bias = jnp.where(live_ref[PICKS * slot] > 0, 0.0, -jnp.inf)
        second_bias = jnp.where(live_ref[PICKS * slot + 1] > 0, 0.0, -jnp.inf)
        first_block = received_ref[slot_ref[PICKS * slot]]
        second_block = received_ref[slot_ref[PICKS * slot + 1]]
        half = rows // 2
        for part in range(2):
            low = part * half
            width = low + half
            query = q_ref[low:low + half, lanes]

            def scores_against(key_rows, query=query):
                raw = lax.dot_general(query, key_rows, dims, preferred_element_type=jnp.float32)
                return raw * score_scale

            row_index = lax.broadcasted_iota(jnp.int32, (half, width), 0) + low
            col_index = lax.broadcasted_iota(jnp.int32, (half, width), 1)
            own = jnp.where(row_index >= col_index, scores_against(k_ref[:width, lanes]),
                            -jnp.inf)
            first = scores_against(first_block[0]) + first_bias
            second = scores_against(second_block[0]) + second_bias
            row_top = jnp.maximum(
                jnp.maximum(jnp.max(own, axis=1), jnp.max(first, axis=1)),
                jnp.max(second, axis=1),
            )[:, None]
            own = jnp.exp(own - row_top)
            first = jnp.exp(first - row_top)
            second = jnp.exp(second - row_top)
            row_scale = 1.0 / (
                jnp.sum(own, axis=1) + jnp.sum(first, axis=1) + jnp.sum(second, axis=1)
            )[:, None]
            mixed = jnp.dot((own * row_scale).astype(jnp.bfloat16), v_ref[:width, lanes],
                            preferred_element_type=jnp.float32)
            mixed += jnp.dot((first * row_scale).astype(jnp.bfloat16), first_block[1],
                             preferred_element_type=jnp.float32)
            mixed += jnp.dot((second * row_scale).astype(jnp.bfloat16), second_block[1],
                             preferred_element_type=jnp.float32)
            out_buf[slot, low:low + half, :] = mixed.astype(out_buf.dtype)
        relay(slot).start()

    @pl.when(step == steps - 1)
    def _():
        def finish(slot, carry):
            relay(slot).wait_send()
            relay(slot).wait_recv()
            return carry

        lax.fori_loop(0, heads, finish, 0)


def attend_and_pass(slots, live, queries, keys, values, received):
    rows = queries.shape[0]
    per_step = 2
    head_block = pl.BlockSpec((rows, per_step * HD), lambda h, slot_ref, live_ref: (0, h))
    grid_spec = pltpu.PrefetchScalarGridSpec(
        num_scalar_prefetch=2,
        grid=(HEADS // per_step,),
        in_specs=[
            head_block,
            head_block,
            head_block,
            pl.BlockSpec(memory_space=pltpu.VMEM),
        ],
        out_specs=pl.BlockSpec(memory_space=pl.ANY),
        scratch_shapes=[
            pltpu.VMEM((HEADS, rows, HD), queries.dtype),
            pltpu.SemaphoreType.DMA((2, HEADS)),
        ],
    )
    return pl.pallas_call(
        attend_kernel,
        grid_spec=grid_spec,
        out_shape=jax.ShapeDtypeStruct(queries.shape, queries.dtype),
        compiler_params=pltpu.CompilerParams(
            collective_id=0, has_side_effects=True, vmem_limit_bytes=48 * 1024 * 1024
        ),
    )(slots, live, queries, keys, values, received)


def per_device(queries, keys, values, picks):
    rank_here = lax.axis_index("ctx")
    every_pick = picks[0]
    head_ids = lax.broadcasted_iota(jnp.int32, every_pick.shape, 1)
    asked = jnp.sum(jnp.where(every_pick == rank_here, head_ids, 0), axis=(1, 2))
    send = pack_requested(asked.astype(jnp.int32), keys[0], values[0])
    received = lax.all_to_all(send, "ctx", split_axis=0, concat_axis=0, tiled=True)
    chosen = lax.dynamic_index_in_dim(every_pick, rank_here, 0, keepdims=False).reshape(-1)
    live = (chosen >= 0).astype(jnp.int32)
    slots = jnp.maximum(chosen, 0).astype(jnp.int32)
    merged = attend_and_pass(slots, live, queries[0], keys[0], values[0], received)
    return merged[None]


def solution(mesh):
    placed = (
        P("pipe", "ctx", None),
        P("pipe", "ctx", None),
        P("pipe", "ctx", None),
        P("pipe", None, None, None),
    )
    return jax.shard_map(
        per_device, mesh=mesh, in_specs=placed, out_specs=P("pipe", "ctx", None), check_vma=False
    )
```

```python
import functools

import jax
import jax.numpy as jnp
from jax import lax
from jax.experimental import pallas as pl
from jax.experimental.pallas import tpu as pltpu
from jax.sharding import PartitionSpec as P

HEADS = 16
HD = 128
PICKS = 2
MESH = pl.DeviceIdType.MESH


def passed_along(value, axis, steps):
    count = lax.axis_size(axis)
    pairs = [(source, (source + steps) % count) for source in range(count)]
    return lax.ppermute(value, axis, pairs)


def pack_kernel(group, asked_ref, k_ref, v_ref, out_ref):
    base = pl.program_id(0) * group
    for i in range(group):
        column = pl.multiple_of(asked_ref[base + i] * HD, HD)
        out_ref[i, 0] = k_ref[:, pl.ds(column, HD)]
        out_ref[i, 1] = v_ref[:, pl.ds(column, HD)]


def pack_requested(asked, keys, values):
    count = asked.shape[0]
    rows, width = keys.shape
    group = 8
    whole = pl.BlockSpec((rows, width), lambda g, asked_ref: (0, 0))
    grid_spec = pltpu.PrefetchScalarGridSpec(
        num_scalar_prefetch=1,
        grid=(count // group,),
        in_specs=[whole, whole],
        out_specs=pl.BlockSpec((group, 2, rows, HD), lambda g, asked_ref: (g, 0, 0, 0)),
    )
    return pl.pallas_call(
        functools.partial(pack_kernel, group),
        grid_spec=grid_spec,
        out_shape=jax.ShapeDtypeStruct((count, 2, rows, HD), keys.dtype),
    )(asked, keys, values)


def exchange_kernel(count, send_ref, recv_ref, send_sems, recv_sems):
    me = lax.axis_index("ctx")
    barrier = pltpu.get_barrier_semaphore()

    def greet(step, carry):
        peer = lax.rem(me + step, count)
        pl.semaphore_signal(barrier, 1, device_id={"ctx": peer}, device_id_type=MESH)
        return carry

    lax.fori_loop(1, count, greet, 0)
    pl.semaphore_wait(barrier, count - 1)

    def copy_between(source, target, slot):
        return pltpu.make_async_remote_copy(
            src_ref=send_ref.at[slot],
            dst_ref=recv_ref.at[source],
            send_sem=send_sems.at[slot],
            recv_sem=recv_sems.at[source],
            device_id={"ctx": target},
            device_id_type=MESH,
        )

    def start(step, carry):
        target = me + step

        @pl.when(target < count)
        def _():
            copy_between(me, target, target).start()

        return carry

    lax.fori_loop(1, count, start, 0)

    def finish(peer, carry):
        @pl.when(peer > me)
        def _():
            copy_between(me, peer, peer).wait_send()

        @pl.when(peer < me)
        def _():
            copy_between(peer, peer, peer).wait_recv()

        return carry

    lax.fori_loop(0, count, finish, 0)


def exchange(send):
    count = send.shape[0]
    return pl.pallas_call(
        functools.partial(exchange_kernel, count),
        out_shape=jax.ShapeDtypeStruct(send.shape, send.dtype),
        in_specs=[pl.BlockSpec(memory_space=pl.ANY)],
        out_specs=pl.BlockSpec(memory_space=pl.ANY),
        scratch_shapes=[
            pltpu.SemaphoreType.DMA((count,)),
            pltpu.SemaphoreType.DMA((count,)),
        ],
        compiler_params=pltpu.CompilerParams(collective_id=0, has_side_effects=True),
    )(send)


def attend_kernel(slot_ref, live_ref, q_ref, k_ref, v_ref, received_ref, o_ref, out_buf, sems):
    head = pl.program_id(0)
    heads = pl.num_programs(0)
    rows = q_ref.shape[0]
    pipe_size = lax.axis_size("pipe")
    here = lax.axis_index("pipe")
    after = lax.rem(here + 1, pipe_size)
    before = lax.rem(here + pipe_size - 1, pipe_size)

    @pl.when(head == 0)
    def _():
        barrier = pltpu.get_barrier_semaphore()
        for peer in (before, after):
            pl.semaphore_signal(barrier, 1, device_id={"pipe": peer}, device_id_type=MESH)
        pl.semaphore_wait(barrier, 2)

    def relay(slot, part):
        low = part * (rows // 2)
        return pltpu.make_async_remote_copy(
            src_ref=out_buf.at[slot, pl.ds(low, rows // 2)],
            dst_ref=o_ref.at[pl.ds(low, rows // 2), pl.ds(pl.multiple_of(slot * HD, HD), HD)],
            send_sem=sems.at[0, part, slot],
            recv_sem=sems.at[1, part, slot],
            device_id={"pipe": after},
            device_id_type=MESH,
        )

    score_scale = HD ** (-0.5)
    dims = (((1,), (1,)), ((), ()))
    first_bias = jnp.where(live_ref[PICKS * head] > 0, 0.0, -jnp.inf)
    second_bias = jnp.where(live_ref[PICKS * head + 1] > 0, 0.0, -jnp.inf)
    first_block = received_ref[slot_ref[PICKS * head]]
    second_block = received_ref[slot_ref[PICKS * head + 1]]
    half = rows // 2
    for part in range(2):
        low = part * half
        width = low + half
        query = q_ref[low:low + half, :]

        def scores_against(key_rows, query=query):
            raw = lax.dot_general(query, key_rows, dims, preferred_element_type=jnp.float32)
            return raw * score_scale

        row_index = lax.broadcasted_iota(jnp.int32, (half, width), 0) + low
        col_index = lax.broadcasted_iota(jnp.int32, (half, width), 1)
        own = jnp.where(row_index >= col_index, scores_against(k_ref[:width, :]), -jnp.inf)
        first = scores_against(first_block[0]) + first_bias
        second = scores_against(second_block[0]) + second_bias
        row_top = jnp.maximum(
            jnp.maximum(jnp.max(own, axis=1), jnp.max(first, axis=1)), jnp.max(second, axis=1)
        )[:, None]
        own = jnp.exp(own - row_top)
        first = jnp.exp(first - row_top)
        second = jnp.exp(second - row_top)
        row_scale = 1.0 / (
            jnp.sum(own, axis=1) + jnp.sum(first, axis=1) + jnp.sum(second, axis=1)
        )[:, None]
        mixed = jnp.dot((own * row_scale).astype(jnp.bfloat16), v_ref[:width, :],
                        preferred_element_type=jnp.float32)
        mixed += jnp.dot((first * row_scale).astype(jnp.bfloat16), first_block[1],
                         preferred_element_type=jnp.float32)
        mixed += jnp.dot((second * row_scale).astype(jnp.bfloat16), second_block[1],
                         preferred_element_type=jnp.float32)
        out_buf[head, low:low + half, :] = mixed.astype(out_buf.dtype)
        relay(head, part).start()

    @pl.when(head == heads - 1)
    def _():
        def finish(slot, carry):
            for part in range(2):
                relay(slot, part).wait_send()
                relay(slot, part).wait_recv()
            return carry

        lax.fori_loop(0, heads, finish, 0)


def attend_and_pass(slots, live, queries, keys, values, received):
    rows = queries.shape[0]
    head_block = pl.BlockSpec((rows, HD), lambda h, slot_ref, live_ref: (0, h))
    grid_spec = pltpu.PrefetchScalarGridSpec(
        num_scalar_prefetch=2,
        grid=(HEADS,),
        in_specs=[
            head_block,
            head_block,
            head_block,
            pl.BlockSpec(memory_space=pltpu.VMEM),
        ],
        out_specs=pl.BlockSpec(memory_space=pl.ANY),
        scratch_shapes=[
            pltpu.VMEM((HEADS, rows, HD), queries.dtype),
            pltpu.SemaphoreType.DMA((2, 2, HEADS)),
        ],
    )
    return pl.pallas_call(
        attend_kernel,
        grid_spec=grid_spec,
        out_shape=jax.ShapeDtypeStruct(queries.shape, queries.dtype),
        compiler_params=pltpu.CompilerParams(
            collective_id=0, has_side_effects=True, vmem_limit_bytes=48 * 1024 * 1024
        ),
    )(slots, live, queries, keys, values, received)


def per_device(queries, keys, values, picks):
    rank_here = lax.axis_index("ctx")
    every_pick = picks[0]
    head_ids = lax.broadcasted_iota(jnp.int32, every_pick.shape, 1)
    asked = jnp.sum(jnp.where(every_pick == rank_here, head_ids, 0), axis=(1, 2))
    send = pack_requested(asked.astype(jnp.int32), keys[0], values[0])
    received = lax.all_to_all(send, "ctx", split_axis=0, concat_axis=0, tiled=True)
    chosen = lax.dynamic_index_in_dim(every_pick, rank_here, 0, keepdims=False).reshape(-1)
    live = (chosen >= 0).astype(jnp.int32)
    slots = jnp.maximum(chosen, 0).astype(jnp.int32)
    merged = attend_and_pass(slots, live, queries[0], keys[0], values[0], received)
    return merged[None]


def solution(mesh):
    placed = (
        P("pipe", "ctx", None),
        P("pipe", "ctx", None),
        P("pipe", "ctx", None),
        P("pipe", None, None, None),
    )
    return jax.shard_map(
        per_device, mesh=mesh, in_specs=placed, out_specs=P("pipe", "ctx", None), check_vma=False
    )
```
